128 devices in a mesh: row: 8 (over x, core), col: 16 (over y, z).
Axes of the slice: x: 4, y: 4, z: 4, core: 2. Of those that a mesh axis runs over, the one named last changes fastest.
Arguments:
- tokens: bfloat16 [3584, 4096], P('row', 'col'), may hold values from -6 to 6
- norm_gain: bfloat16 [4096], P('col'), may hold values from 0.25 to 1.75
- w_query: bfloat16 [4096, 4096], P('row', 'col'), as said below
- w_key: bfloat16 [4096, 1024], P('row'), as said below
- w_value: bfloat16 [4096, 1024], P('row'), may hold values from -0.09375 to 0.09375
- w_out: bfloat16 [4096, 4096], P('col', 'row'), may hold values from -0.09375 to 0.09375
- out_grad: bfloat16 [3584, 4096], P('row', 'col'), may hold values from -6 to 6
- doc_lengths: int32 [4], replicated, may hold values from 1 to 1792, 3584 in all
Outputs:
- layer_out: bfloat16 [3584, 4096], P('row', 'col')
- token_grad: float32 [3584, 4096], P('row', 'col')
- gain_grad: float32 [4096], P('col')
- query_weight_grad: float32 [4096, 4096], P('row', 'col')
- key_weight_grad: float32 [4096, 1024], P('row', 'col')
- value_weight_grad: float32 [4096, 1024], P('row', 'col')
- out_weight_grad: float32 [4096, 4096], P('col', 'row')
The draws below stay inside these ranges and needn't reach their ends.
Inputs may be any that keep to these rules, and one draw needn't show every extreme that they name: `doc_lengths`: the lengths of 4 documents packed in order, summing to 3584; the longest is exactly 1792. `w_query`: every entry is at most 7 / sqrt(4096) in magnitude. `w_key`: every entry is at most 7 / sqrt(4096) in magnitude.
All inputs are finite; a program needn't handle non-finite values.
Results may differ from the reference program's by a relative error of at most 0.0045.
The reference program's roundings to bfloat16 on the way (of `normed`, `probs_low`, `attended`, `att_grad` and `score_grad`) count: a program that leaves them out, or rounds other values in their place, can miss the bound.
Values may be sent and summed in bfloat16 or wider, within the bound.
A program may use at most 128 MiB of HBM per device.

```python
import math
import jax
import jax.numpy as jnp
import numpy as np
from jax import lax

D = 4096
HEADS = 32
KV_HEADS = 8
HEAD_DIM = 128
DOCS = 4
TOKENS = 3584
MOST_DOC = 1792


def draw_tokens(key, part):
    own_key = jax.random.fold_in(key, 11)
    values = jnp.clip(jax.random.normal(own_key, (TOKENS, D), jnp.float32), -6.0, 6.0)
    return values.astype(jnp.bfloat16)


def draw_w_query(key, part):
    own_key = jax.random.fold_in(key, 12)
    unit_scale = D ** (-0.5)
    weights = jnp.clip(jax.random.normal(own_key, (D, HEADS * HEAD_DIM), jnp.float32), -6.0, 6.0) * unit_scale
    return weights.astype(jnp.bfloat16)


def draw_w_key(key, part):
    own_key = jax.random.fold_in(key, 13)
    unit_scale = D ** (-0.5)
    weights = jnp.clip(jax.random.normal(own_key, (D, KV_HEADS * HEAD_DIM), jnp.float32), -6.0, 6.0) * unit_scale
    return weights.astype(jnp.bfloat16)


def steps_of(key, dims, cuts, low, largest):
    loudness, own = 1.0, jax.random.fold_in(key, 6)
    for position, shards_of in cuts:
        steps = jnp.exp(jax.random.uniform(jax.random.fold_in(own, position), (shards_of,), jnp.float32, low / len(cuts), largest / len(cuts)))
        loudness = loudness * jnp.repeat(steps, dims[position] // shards_of).reshape([-1 if axis == position else 1 for axis in range(len(dims))])
    return loudness


def length_profile(count, total, most, slope):
    portions = [(1 << 20) // math.isqrt(standing ** slope) + 1 for standing in range(2, count + 1)]
    surplus, counts = total - most - (count - 1), [1] * (count - 1)
    while surplus > 0:
        free = [i for i in range(count - 1) if counts[i] < most]
        mass, budget = sum([portions[i] for i in free]), surplus
        for i in free:
            extra = min(most - counts[i], max(1, budget * portions[i] // mass), surplus)
            counts[i] = counts[i] + extra
            surplus = surplus - extra
    return np.array([most] + counts)


def uneven(rng, amount, total, most, lean):
    if amount == 2:
        one = jax.random.randint(rng, (), max(1, total - most), min(most, total - 1) + 1)
        return jnp.stack([one, total - one])
    sizes = jnp.asarray(length_profile(amount, total, most, lean), jnp.int32)
    twos = (amount - 1) // 2
    source_of, taker = sizes[1:1 + 2 * twos:2], sizes[2:2 + 2 * twos:2]
    margin = jnp.minimum(source_of - 1, most - taker)
    shifted = jax.random.randint(jax.random.fold_in(rng, 1), (twos,), 0, 1 << 20) % (margin + 1)
    sizes = sizes.at[1:1 + 2 * twos:2].set(source_of - shifted).at[2:2 + 2 * twos:2].set(taker + shifted)
    return sizes[jax.random.permutation(jax.random.fold_in(rng, 2), amount)]


def bell_draw(stream_key, dims, deviation, bound, cuts=(), held_as=jnp.bfloat16):
    values = deviation * jax.random.normal(stream_key, dims, jnp.float32)
    if cuts:
        values = values * steps_of(stream_key, dims, cuts, -0.22, 0.18)
    return jnp.clip(values, -bound, bound).astype(held_as)


def setup_inputs(seed: int = 0) -> dict:
    splits = jax.random.split(jax.random.key(seed), 9)
    tokens = draw_tokens(jax.random.fold_in(splits[8], 71), 0)
    norm_gain = jnp.clip(1.0 + 0.15 * jax.random.normal(splits[1], (D,), jnp.float32), 0.25, 1.75).astype(jnp.bfloat16)
    w_query = draw_w_query(jax.random.fold_in(splits[8], 71), 0)
    w_key = draw_w_key(jax.random.fold_in(splits[8], 71), 0)
    w_value = bell_draw(splits[4], (D, KV_HEADS * HEAD_DIM), D ** -0.5, 0.09375, ((0, 8),))
    w_out = bell_draw(splits[5], (HEADS * HEAD_DIM, D), (HEADS * HEAD_DIM) ** -0.5, 0.09375, ((0, 16), (1, 8)))
    out_grad = bell_draw(splits[6], (TOKENS, D), 1.0, 6.0, ((0, 8), (1, 16)))
    doc_lengths = uneven(splits[7], DOCS, TOKENS, MOST_DOC, 2).astype(jnp.int32)
    return {"tokens": tokens, "norm_gain": norm_gain, "w_query": w_query, "w_key": w_key, "w_value": w_value, "w_out": w_out, "out_grad": out_grad, "doc_lengths": doc_lengths}


eps = 1e-05

def doc_index(positions, doc_lengths):
    ends = jnp.cumsum(doc_lengths).astype(jnp.int32)
    return lax.optimization_barrier(jnp.sum((positions[:, None] >= ends[None, :]).astype(jnp.int32), axis=1))

def masked_probs(query_head, key_head, allowed):
    scores = jnp.dot(query_head, key_head.T, preferred_element_type=jnp.float32) * HEAD_DIM ** (-0.5)
    scores = jnp.where(allowed, scores, -1e+30)
    row_max = lax.optimization_barrier(jnp.max(scores, axis=-1, keepdims=True))
    expo_scores = jnp.exp(scores - row_max)
    return expo_scores / lax.optimization_barrier(jnp.sum(expo_scores, axis=-1, keepdims=True))

def by_head(matrix, head_count):
    return matrix.reshape(TOKENS, head_count, HEAD_DIM).transpose(1, 0, 2)

def by_token(stacked):
    return stacked.transpose(1, 0, 2).reshape(TOKENS, HEADS * HEAD_DIM)

def reference(tokens, norm_gain, w_query, w_key, w_value, w_out, out_grad, doc_lengths):
    widened = tokens.astype(jnp.float32)
    gain_wide = norm_gain.astype(jnp.float32)
    inverse = lax.rsqrt(lax.optimization_barrier(jnp.mean(widened * widened, axis=1, keepdims=True)) + eps)
    normed = (widened * inverse * gain_wide).astype(jnp.bfloat16)
    query_local = jnp.dot(normed, w_query, preferred_element_type=jnp.float32).astype(jnp.bfloat16)
    key_local = jnp.dot(normed, w_key, preferred_element_type=jnp.float32).astype(jnp.bfloat16)
    value_local = jnp.dot(normed, w_value, preferred_element_type=jnp.float32).astype(jnp.bfloat16)
    att_grad = jnp.dot(out_grad, w_out.T, preferred_element_type=jnp.float32).astype(jnp.bfloat16)
    group_size = HEADS // KV_HEADS
    query_heads = by_head(query_local, HEADS)
    key_heads = jnp.repeat(by_head(key_local, KV_HEADS), group_size, axis=0)
    value_heads = jnp.repeat(by_head(value_local, KV_HEADS), group_size, axis=0)
    grad_heads = by_head(att_grad, HEADS)
    positions = jnp.arange(TOKENS, dtype=jnp.int32)
    doc_ids = doc_index(positions, doc_lengths)
    allowed = (positions[None, :] <= positions[:, None]) & (doc_ids[None, :] == doc_ids[:, None])

    def one_head(head_items):
        query_head, key_head, value_head, grad_head = head_items
        soft_probs = masked_probs(query_head, key_head, allowed)
        probs_low = soft_probs.astype(jnp.bfloat16)
        attended_head = jnp.dot(probs_low, value_head, preferred_element_type=jnp.float32).astype(jnp.bfloat16)
        prob_grad = jnp.dot(grad_head, value_head.T, preferred_element_type=jnp.float32)
        weighted = lax.optimization_barrier(jnp.sum(soft_probs * prob_grad, axis=-1, keepdims=True))
        score_grad = (soft_probs * (prob_grad - weighted) * HEAD_DIM ** (-0.5)).astype(jnp.bfloat16)
        query_part = jnp.dot(score_grad, key_head, preferred_element_type=jnp.float32).astype(jnp.bfloat16)
        key_part = jnp.dot(score_grad.T, query_head, preferred_element_type=jnp.float32).astype(jnp.bfloat16)
        value_part = jnp.dot(probs_low.T, grad_head, preferred_element_type=jnp.float32).astype(jnp.bfloat16)
        return (attended_head, query_part, key_part, value_part)
    attended, d_query, d_keys, d_values = lax.map(one_head, (query_heads, key_heads, value_heads, grad_heads))
    attended = by_token(attended)
    d_query = by_token(d_query)
    d_keys = by_token(d_keys)
    d_values = by_token(d_values)
    mixed_rows = jnp.dot(attended, w_out, preferred_element_type=jnp.float32)
    layer_out = (widened + mixed_rows).astype(jnp.bfloat16)
    out_weight_grad = jnp.dot(attended.T, out_grad, preferred_element_type=jnp.float32)
    key_tiled = jnp.repeat(w_key.reshape(D, KV_HEADS, HEAD_DIM), group_size, axis=1).reshape(D, HEADS * HEAD_DIM)
    value_tiled = jnp.repeat(w_value.reshape(D, KV_HEADS, HEAD_DIM), group_size, axis=1).reshape(D, HEADS * HEAD_DIM)
    normed_grad = jnp.dot(d_query, w_query.T, preferred_element_type=jnp.float32) + jnp.dot(d_keys, key_tiled.T, preferred_element_type=jnp.float32) + jnp.dot(d_values, value_tiled.T, preferred_element_type=jnp.float32)
    query_weight_grad = jnp.dot(normed.T, d_query, preferred_element_type=jnp.float32)
    key_weight_grad = jnp.dot(normed.T, d_keys, preferred_element_type=jnp.float32).reshape(D, KV_HEADS, group_size, HEAD_DIM).sum(axis=2).reshape(D, KV_HEADS * HEAD_DIM)
    value_weight_grad = jnp.dot(normed.T, d_values, preferred_element_type=jnp.float32).reshape(D, KV_HEADS, group_size, HEAD_DIM).sum(axis=2).reshape(D, KV_HEADS * HEAD_DIM)
    scaled_grad = normed_grad * gain_wide[None, :]
    inner_mean = lax.optimization_barrier(jnp.mean(scaled_grad * widened, axis=1, keepdims=True))
    token_grad = out_grad.astype(jnp.float32) + inverse * scaled_grad - widened * inverse ** 3 * inner_mean
    gain_grad = lax.optimization_barrier(jnp.sum(normed_grad * widened * inverse, axis=0))
    return (layer_out, token_grad, gain_grad, query_weight_grad, key_weight_grad, value_weight_grad, out_weight_grad)
```

```python
import functools

import jax
import jax.numpy as jnp
from jax import lax
from jax.experimental import pallas as pl
from jax.experimental.pallas import tpu as pltpu
from jax.sharding import PartitionSpec as P

HEAD_DIM = 128
BLOCK = 448
EXTRA = 16
WIDTH = 256
TILE = 256
MOST_TILES = 10
eps = 1e-05
FACTOR = HEAD_DIM ** (-0.5)
F32 = jnp.float32
BF16 = jnp.bfloat16
ANY = pl.BlockSpec(memory_space=pl.ANY)
VM = pl.BlockSpec(memory_space=pltpu.VMEM)
VMEM_MOST = 60 * 1024 * 1024


class Net:
    def __init__(self, send, recv):
        self.send, self.recv, self.used, self.open = send, recv, 0, []
        self.r, self.c = lax.axis_index("row"), lax.axis_index("col")
        self.x, self.k = self.r // 2, lax.rem(self.r, 2)
        self.y, self.z = self.c // 4, lax.rem(self.c, 4)

    def dev(self, axis, step=1):
        if axis == "k":
            return (self.x * 2 + 1 - self.k, self.c)
        if axis == "x":
            return (lax.rem(self.x + step + 4, 4) * 2 + self.k, self.c)
        if axis == "y":
            return (self.r, self.col(step, 0))
        return (self.r, self.col(0, step))

    def col(self, dy, dz):
        return lax.rem(self.y + dy + 4, 4) * 4 + lax.rem(self.z + dz + 4, 4)

    def greet(self, devices):
        bar = pltpu.get_barrier_semaphore()
        for d in devices:
            pl.semaphore_signal(bar, inc=1, device_id=d, device_id_type=pl.DeviceIdType.MESH)
        pl.semaphore_wait(bar, len(devices))

    def push(self, src, dst, device):
        i = self.used
        self.used += 1
        copy = pltpu.make_async_remote_copy(
            src_ref=src, dst_ref=dst, send_sem=self.send.at[i], recv_sem=self.recv.at[i],
            device_id=device, device_id_type=pl.DeviceIdType.MESH)
        copy.start()
        self.open.append(copy)
        return copy

    def finish(self):
        for copy in self.open:
            copy.wait_send()


def run(streams):
    streams = list(streams)
    while streams:
        left = []
        for s in streams:
            try:
                next(s)
                left.append(s)
            except StopIteration:
                pass
        streams = left


def gather_plane(net, own, at, low, count, half, first):
    second = "z" if first == "y" else "y"

    def blk(da, db, lo=low, n=count):
        dy, dz = (da, db) if first == "y" else (db, da)
        return at(net.col(dy, dz), lo, n)

    t0, tn = low, half
    b0, bn = low + half, count - half
    mine = own(low, count)
    ar = net.push(mine, blk(0, 0), net.dev(first, 1))
    al = net.push(mine, blk(0, 0), net.dev(first, -1))
    br = {0: net.push(mine, blk(0, 0), net.dev(second, 1))}
    bl = {0: net.push(mine, blk(0, 0), net.dev(second, -1))}
    tail = []

    def send_unit(u):
        br[u] = net.push(blk(u, 0), blk(u, 0), net.dev(second, 1))
        bl[u] = net.push(blk(u, 0), blk(u, 0), net.dev(second, -1))

    def relay_unit(u):
        br[u].wait_recv()
        tail.append(net.push(blk(u, -1, t0, tn), blk(u, -1, t0, tn), net.dev(second, 1)))
        bl[u].wait_recv()
        tail.append(net.push(blk(u, 1, b0, bn), blk(u, 1, b0, bn), net.dev(second, -1)))

    yield
    ar.wait_recv()
    fr = net.push(blk(-1, 0, t0, tn), blk(-1, 0, t0, tn), net.dev(first, 1))
    send_unit(-1)
    al.wait_recv()
    fl = net.push(blk(1, 0, b0, bn), blk(1, 0, b0, bn), net.dev(first, -1))
    send_unit(1)
    yield
    relay_unit(0)
    yield
    fr.wait_recv()
    fl.wait_recv()
    send_unit(2)
    yield
    relay_unit(-1)
    relay_unit(1)
    yield
    relay_unit(2)
    yield
    for copy in tail:
        copy.wait_recv()


def gather_row(net, parts, at, half):
    sent = [[net.push(s, d, net.dev(a, e)) for s, d in parts] for a, e in (("x", 1), ("x", -1), ("k", 1))]

    def blk(dx, lo=0, n=None):
        return at(lax.rem(net.x + dx + 4, 4) * 2 + net.k, lo, n)

    yield
    for c in sent[0]:
        c.wait_recv()
    fr = net.push(blk(-1, 0, half), blk(-1, 0, half), net.dev("x", 1))
    tail = [net.push(blk(-1), blk(-1), net.dev("k"))]
    for c in sent[1]:
        c.wait_recv()
    fl = net.push(blk(1, half, half), blk(1, half, half), net.dev("x", -1))
    tail.append(net.push(blk(1), blk(1), net.dev("k")))
    yield
    yield
    fr.wait_recv()
    tail.append(net.push(blk(2, 0, half), blk(2, 0, half), net.dev("k")))
    fl.wait_recv()
    tail.append(net.push(blk(2, half, half), blk(2, half, half), net.dev("k")))
    yield
    yield
    for c in sent[2] + tail:
        c.wait_recv()


def stage(moves, sems, base):
    legs = []
    for i, (src, buf, _) in enumerate(moves):
        legs.append(pltpu.make_async_copy(src, buf, sems.at[base + 2 * i]))
        legs[-1].start()
    outs = []
    for i, (_, buf, dsts) in enumerate(moves):
        legs[i].wait()
        outs.append(pltpu.make_async_copy(buf, dsts, sems.at[base + 2 * i + 1]))
        outs[-1].start()
    return outs


def gather_kernel(tok, grad, wq, wk, wv, wo, tok3, grad3, wqkv, wo3,
                  b_tok, b_grad, b_q, b_k, b_v, b_o, send, recv, here):
    net = Net(send, recv)
    net.greet([net.dev("y", 1), net.dev("y", -1), net.dev("z", 1), net.dev("z", -1),
               net.dev("x", 1), net.dev("x", -1), net.dev("k")])
    r, c = net.r, net.c
    slot = pl.multiple_of(c // 2 * HEAD_DIM, HEAD_DIM)
    wk_own, wv_own = wk.at[:, pl.ds(slot, HEAD_DIM)], wv.at[:, pl.ds(slot, HEAD_DIM)]
    q_at, k_at, v_at = (wqkv.at[r, :, pl.ds(0, 256)], wqkv.at[r, :, pl.ds(256, 128)],
                        wqkv.at[r, :, pl.ds(384, 128)])

    def at3(ref):
        return lambda i, lo, n: ref.at[i, pl.ds(lo, n)]

    def whole(ref, rows):
        return lambda i, lo, n: ref.at[i, pl.ds(lo, rows if n is None else n)]

    def own(ref):
        return lambda lo, n: ref.at[pl.ds(lo, n)]

    streams = [
        gather_plane(net, own(tok), at3(tok3), 0, 224, 112, "y"),
        gather_plane(net, own(tok), at3(tok3), 224, 240, 112, "z"),
        gather_row(net, [(wq, q_at), (wk_own, k_at), (wv_own, v_at)], whole(wqkv, 512), 256),
        gather_row(net, [(wo, wo3.at[r])], whole(wo3, 256), 128),
        gather_plane(net, own(grad), at3(grad3), 0, 224, 112, "y"),
        gather_plane(net, own(grad), at3(grad3), 224, 224, 112, "z"),
    ]
    for s in streams:
        next(s)
    outs = stage([(tok, b_tok, tok3.at[c]), (grad, b_grad, grad3.at[c]), (wq, b_q, q_at),
                  (wk_own, b_k, k_at), (wv_own, b_v, v_at), (wo, b_o, wo3.at[r])], here, 0)
    run(streams)
    for o in outs:
        o.wait()
    net.finish()


def gather_all(tok, grad, wq, wk, wv, wo):
    rows = tok.shape[0]
    copies = 2 * 2 * 20 + 15 + 9
    return pl.pallas_call(
        gather_kernel,
        out_shape=(
            jax.ShapeDtypeStruct((16, rows, WIDTH), BF16),
            jax.ShapeDtypeStruct((16, BLOCK, WIDTH), BF16),
            jax.ShapeDtypeStruct((8, 512, 512), BF16),
            jax.ShapeDtypeStruct((8, 256, 512), BF16),
        ),
        in_specs=[ANY] * 6,
        out_specs=(ANY,) * 4,
        scratch_shapes=[
            pltpu.VMEM((rows, WIDTH), BF16), pltpu.VMEM((BLOCK, WIDTH), BF16),
            pltpu.VMEM((512, 256), BF16), pltpu.VMEM((512, 128), BF16), pltpu.VMEM((512, 128), BF16),
            pltpu.VMEM((256, 512), BF16),
            pltpu.SemaphoreType.DMA((copies,)), pltpu.SemaphoreType.DMA((copies,)),
            pltpu.SemaphoreType.DMA((12,)),
        ],
        compiler_params=pltpu.CompilerParams(collective_id=1, has_side_effects=True),
        name="gather_all",
    )(tok, grad, wq, wk, wv, wo)


def project_kernel(tok, grad, wqkv, wo, normed, pack, inverse, sums, inv, grads, qkv):
    phase, c = pl.program_id(0), pl.program_id(1)
    nt = (((1,), (1,)), ((), ()))

    @pl.when(phase == 0)
    def _():
        t = tok[0, :BLOCK, :].astype(F32)
        t = t * t
        t = t[:, :128] + t[:, 128:]
        g = lax.dot_general(grad[0], wo[0], nt, preferred_element_type=F32)

        @pl.when(c == 0)
        def _():
            sums[...] = t
            grads[...] = g

        @pl.when(c > 0)
        def _():
            sums[...] += t
            grads[...] += g

    @pl.when(phase == 1)
    def _():
        @pl.when(c == 0)
        def _():
            s = jnp.sum(sums[...], axis=1, keepdims=True)
            i = lax.rsqrt(s * (1.0 / 4096) + eps)
            inv[...] = jnp.broadcast_to(i, inv.shape)
            inverse[...] = i

        i = inv[...]
        t = tok[0, :BLOCK, :].astype(F32) * jnp.concatenate([i, i], axis=1)
        n = (t * tok[0, BLOCK:BLOCK + 1, :].astype(F32)).astype(BF16)
        normed[0] = n
        d = jnp.dot(n, wqkv[...], preferred_element_type=F32)

        @pl.when(c == 0)
        def _():
            qkv[...] = d

        @pl.when(c > 0)
        def _():
            qkv[...] += d

        @pl.when(c == 15)
        def _():
            pack[:, :256] = qkv[:, :256].astype(BF16)
            pack[:, 256:512] = grads[...].astype(BF16)
            pack[:, 512:] = qkv[:, 256:].astype(BF16)


def project(tok3, grad3, wqkv, wo3):
    rows = tok3.shape[1]
    return pl.pallas_call(
        project_kernel,
        grid=(2, 16),
        out_shape=(
            jax.ShapeDtypeStruct((16, BLOCK, WIDTH), BF16),
            jax.ShapeDtypeStruct((BLOCK, 768), BF16),
            jax.ShapeDtypeStruct((BLOCK, 1), F32),
        ),
        in_specs=[
            pl.BlockSpec((1, rows, WIDTH), lambda p, c: (c, 0, 0)),
            pl.BlockSpec((1, BLOCK, WIDTH), lambda p, c: (c * (1 - p) + 15 * p, 0, 0)),
            pl.BlockSpec((256, 512), lambda p, c: (c * p, 0)),
            pl.BlockSpec((1, 256, 256), lambda p, c: ((c * (1 - p) + 15 * p) // 2, 0, (c * (1 - p) + 15 * p) % 2)),
        ],
        out_specs=(
            pl.BlockSpec((1, BLOCK, WIDTH), lambda p, c: (c * p, 0, 0)),
            pl.BlockSpec((BLOCK, 768), lambda p, c: (0, 0)),
            pl.BlockSpec((BLOCK, 1), lambda p, c: (0, 0)),
        ),
        scratch_shapes=[pltpu.VMEM((BLOCK, 128), F32), pltpu.VMEM((BLOCK, 128), F32),
                        pltpu.VMEM((BLOCK, 256), F32), pltpu.VMEM((BLOCK, 512), F32)],
        compiler_params=pltpu.CompilerParams(vmem_limit_bytes=VMEM_MOST),
        name="project",
    )(tok3, grad3, wqkv, wo3)


def share_kernel(pack, out, buf, send, recv, here):
    net = Net(send, recv)
    net.greet([net.dev("x", 1), net.dev("x", -1), net.dev("k")])
    own = out.at[net.r]
    stream = gather_row(net, [(pack, own)], lambda i, lo, n: out.at[i, pl.ds(lo, BLOCK if n is None else n)], 224)
    next(stream)
    outs = stage([(pack, buf, own)], here, 0)
    run([stream])
    for o in outs:
        o.wait()
    net.finish()


def share(pack):
    return pl.pallas_call(
        share_kernel,
        out_shape=jax.ShapeDtypeStruct((8, BLOCK, 768), BF16),
        in_specs=[ANY],
        out_specs=ANY,
        scratch_shapes=[pltpu.VMEM((BLOCK, 768), BF16), pltpu.SemaphoreType.DMA((9,)),
                        pltpu.SemaphoreType.DMA((9,)), pltpu.SemaphoreType.DMA((2,))],
        compiler_params=pltpu.CompilerParams(collective_id=2, has_side_effects=True),
        name="share",
    )(pack)


NT = (((1,), (1,)), ((), ()))


def fold(a):
    return a[:, :128] + a[:, 128:]


def query_kernel(bounds, start, pack, att, dq, stats, s_all, dp_all, m_part, l_part, w_part, a_sum, q_sum):
    r, low, count = bounds[0], bounds[1], bounds[2]
    base = pl.multiple_of(r * BLOCK, 64)
    spot = base + lax.broadcasted_iota(jnp.int32, (BLOCK, 1), 0)
    first = start[...]
    lane = lax.broadcasted_iota(jnp.int32, (BLOCK, 128), 1)
    table = jnp.zeros((BLOCK, 128), F32)
    for h in range(2):
        q = pack[pl.ds(base, BLOCK), h * 128:(h + 1) * 128]
        g = pack[pl.ds(base, BLOCK), 256 + h * 128:256 + (h + 1) * 128]
        m_part[...] = jnp.full_like(m_part, -1e30)
        l_part[...] = jnp.zeros_like(l_part)
        w_part[...] = jnp.zeros_like(w_part)
        a_sum[...] = jnp.zeros_like(a_sum)
        q_sum[...] = jnp.zeros_like(q_sum)

        def rows(i):
            return pl.ds(pl.multiple_of((low + i) * TILE, TILE), TILE)

        @pl.loop(0, count)
        def _(i):
            s = lax.dot_general(q, pack[rows(i), 512:640], NT, preferred_element_type=F32) * FACTOR
            key = (low + i) * TILE + lax.broadcasted_iota(jnp.int32, (1, TILE), 1)
            s = jnp.where((key <= spot) & (key >= first), s, -1e30)
            s_all[i] = s
            m_part[...] = jnp.maximum(m_part[...], jnp.maximum(s[:, :128], s[:, 128:]))

        m = jnp.max(m_part[...], axis=1, keepdims=True)

        @pl.loop(0, count)
        def _(i):
            e = jnp.exp(s_all[i] - m)
            dp = lax.dot_general(g, pack[rows(i), 640:768], NT, preferred_element_type=F32)
            s_all[i] = e
            dp_all[i] = dp
            l_part[...] += fold(e)
            w_part[...] += fold(e * dp)

        inv = 1.0 / jnp.sum(l_part[...], axis=1, keepdims=True)
        w = jnp.sum(w_part[...], axis=1, keepdims=True) * inv

        @pl.loop(0, count)
        def _(i):
            p = s_all[i] * inv
            d = (p * (dp_all[i] - w) * FACTOR).astype(BF16)
            a_sum[...] += jnp.dot(p.astype(BF16), pack[rows(i), 640:768], preferred_element_type=F32)
            q_sum[...] += jnp.dot(d, pack[rows(i), 512:640], preferred_element_type=F32)

        att[:, h * 128:(h + 1) * 128] = a_sum[...].astype(BF16)
        dq[:, h * 128:(h + 1) * 128] = q_sum[...].astype(BF16)
        for j, v in enumerate((m, inv, w)):
            table = jnp.where(lane == 3 * h + j, v, table)
    stats[...] = table


SMEM = pl.BlockSpec(memory_space=pltpu.SMEM)


def query_side(bounds, start, pack):
    return pl.pallas_call(
        query_kernel,
        out_shape=(jax.ShapeDtypeStruct((BLOCK, 256), BF16), jax.ShapeDtypeStruct((BLOCK, 256), BF16),
                   jax.ShapeDtypeStruct((BLOCK, 128), F32)),
        in_specs=[SMEM, VM, VM],
        out_specs=(VM, VM, VM),
        scratch_shapes=[pltpu.VMEM((MOST_TILES, BLOCK, TILE), F32)] * 2 + [pltpu.VMEM((BLOCK, 128), F32)] * 5,
        compiler_params=pltpu.CompilerParams(vmem_limit_bytes=VMEM_MOST),
        name="query_side",
    )(bounds, start, pack)


def key_kernel(bounds, start, stats, pack, out, k_sum, v_sum):
    r, low, count = bounds[0], bounds[3], bounds[4]
    base = pl.multiple_of(r * BLOCK, 64)
    key = base + lax.broadcasted_iota(jnp.int32, (BLOCK, 1), 0)
    k = pack[pl.ds(base, BLOCK), 512:640]
    v = pack[pl.ds(base, BLOCK), 640:768]
    for h in range(2):
        k_sum[...] = jnp.zeros_like(k_sum)
        v_sum[...] = jnp.zeros_like(v_sum)

        @pl.loop(0, count)
        def _(i):
            at = pl.ds(pl.multiple_of((low + i) * TILE, TILE), TILE)
            q = pack[at, h * 128:(h + 1) * 128]
            g = pack[at, 256 + h * 128:256 + (h + 1) * 128]
            m, inv, w = (stats[3 * h + j:3 * h + j + 1, at] for j in range(3))
            spot = (low + i) * TILE + lax.broadcasted_iota(jnp.int32, (1, TILE), 1)
            s = lax.dot_general(k, q, NT, preferred_element_type=F32) * FACTOR
            s = jnp.where((key <= spot) & (key >= start[0:1, at]), s, -1e30)
            p = jnp.exp(s - m) * inv
            dp = lax.dot_general(v, g, NT, preferred_element_type=F32)
            d = (p * (dp - w) * FACTOR).astype(BF16)
            v_sum[...] += jnp.dot(p.astype(BF16), g, preferred_element_type=F32)
            k_sum[...] += jnp.dot(d, q, preferred_element_type=F32)

        out[:, h * 128:(h + 1) * 128] = k_sum[...].astype(BF16)
        out[:, 256 + h * 128:256 + (h + 1) * 128] = v_sum[...].astype(BF16)


def key_side(bounds, start, stats, pack):
    return pl.pallas_call(
        key_kernel,
        out_shape=jax.ShapeDtypeStruct((BLOCK, 512), BF16),
        in_specs=[SMEM, VM, VM, VM],
        out_specs=VM,
        scratch_shapes=[pltpu.VMEM((BLOCK, 128), F32)] * 2,
        compiler_params=pltpu.CompilerParams(vmem_limit_bytes=VMEM_MOST),
        name="key_side",
    )(bounds, start, stats, pack)


def stats_kernel(own, out, send, recv, here):
    net = Net(send, recv)
    peers = [(lax.rem(net.r + d, 8), net.c) for d in range(1, 8)]
    net.greet(peers)
    copies = [net.push(own, out.at[net.r], p) for p in peers]
    local = pltpu.make_async_copy(own, out.at[net.r], here.at[0])
    local.start()
    for copy in copies:
        copy.wait_recv()
    local.wait()
    net.finish()


def share_stats(own):
    return pl.pallas_call(
        stats_kernel,
        out_shape=jax.ShapeDtypeStruct((8, 8, BLOCK), F32),
        in_specs=[VM],
        out_specs=VM,
        scratch_shapes=[pltpu.SemaphoreType.DMA((7,)), pltpu.SemaphoreType.DMA((7,)),
                        pltpu.SemaphoreType.DMA((1,))],
        compiler_params=pltpu.CompilerParams(collective_id=3, has_side_effects=True),
        name="share_stats",
    )(own)


def pair_kernel(own, out, send, recv):
    net = Net(send, recv)
    other = (net.r, net.c + 1 - 2 * lax.rem(net.c, 2))
    net.greet([other])
    net.push(own, out, other).wait_recv()
    net.finish()


def swap_pair(own):
    return pl.pallas_call(
        pair_kernel,
        out_shape=jax.ShapeDtypeStruct(own.shape, own.dtype),
        in_specs=[VM],
        out_specs=VM,
        scratch_shapes=[pltpu.SemaphoreType.DMA((1,)), pltpu.SemaphoreType.DMA((1,))],
        compiler_params=pltpu.CompilerParams(collective_id=4, has_side_effects=True),
        name="swap_pair",
    )(own)


def parts_kernel(att, dq, dkv, inverse, tok, wqkv, wo, mix, ngrad, gain, inner):
    c = pl.program_id(0)
    mix[0] = jnp.dot(att[...], wo[0], preferred_element_type=F32).astype(BF16)
    g = lax.dot_general(dq[...], wqkv[:, :256], NT, preferred_element_type=F32)
    for j in range(4):
        side = 256 + 128 * (j // 2)
        g += lax.dot_general(dkv[:, j * 128:(j + 1) * 128], wqkv[:, side:side + 128], NT,
                             preferred_element_type=F32)
    ngrad[0] = g.astype(BF16)
    a = g * tok[0, :BLOCK, :].astype(F32)
    b = fold(a * tok[0, BLOCK:BLOCK + 1, :].astype(F32))
    gain[0] = jnp.sum((a * inverse[...]).reshape(BLOCK // 8, 8, WIDTH), axis=0)

    @pl.when(c == 0)
    def _():
        inner[...] = b

    @pl.when(c > 0)
    def _():
        inner[...] += b


def parts(att, dq, dkv, inverse, tok3, wqkv, wo3):
    rows = tok3.shape[1]
    full = lambda *s: pl.BlockSpec(s, lambda c: (0,) * len(s))
    return pl.pallas_call(
        parts_kernel,
        grid=(16,),
        out_shape=(jax.ShapeDtypeStruct((16, BLOCK, WIDTH), BF16), jax.ShapeDtypeStruct((16, BLOCK, WIDTH), BF16),
                   jax.ShapeDtypeStruct((16, 8, WIDTH), F32), jax.ShapeDtypeStruct((BLOCK, 128), F32)),
        in_specs=[full(BLOCK, 256), full(BLOCK, 256), full(BLOCK, 512), full(BLOCK, 1),
                  pl.BlockSpec((1, rows, WIDTH), lambda c: (c, 0, 0)),
                  pl.BlockSpec((256, 512), lambda c: (c, 0)),
                  pl.BlockSpec((1, 256, 256), lambda c: (c // 2, 0, c % 2))],
        out_specs=(pl.BlockSpec((1, BLOCK, WIDTH), lambda c: (c, 0, 0)),
                   pl.BlockSpec((1, BLOCK, WIDTH), lambda c: (c, 0, 0)),
                   pl.BlockSpec((1, 8, WIDTH), lambda c: (c, 0, 0)),
                   full(BLOCK, 128)),
        compiler_params=pltpu.CompilerParams(vmem_limit_bytes=VMEM_MOST),
        name="parts",
    )(att, dq, dkv, inverse, tok3, wqkv, wo3)


def scatter_plane(net, src, acc, q_top, q_low, f_next, f_prev, low, count, half, first, out):
    second = "z" if first == "y" else "y"

    def mine(da, db, lo, n):
        dy, dz = (db, da) if first == "y" else (da, db)
        return src[net.col(dy, dz), pl.ds(low + lo, n), :]

    def mine_at(da, db, lo, n):
        dy, dz = (db, da) if first == "y" else (da, db)
        return src.at[net.col(dy, dz), pl.ds(low + lo, n)]

    rest = count - half
    units = (2, -1, 1, 0)
    tops, lows, nexts, prevs = {}, {}, {}, {}
    for i, u in enumerate(units):
        tops[u] = net.push(mine_at(u, 2, 0, half), q_top.at[i, pl.ds(0, half)], net.dev(first, -1))
        lows[u] = net.push(mine_at(u, 2, half, rest), q_low.at[i, pl.ds(0, rest)], net.dev(first, 1))
    yield
    for i, u in enumerate(units):
        tops[u].wait_recv()
        acc[0, i, :half] = (mine(u, -1, 0, half).astype(F32) + q_top[i, :half].astype(F32)).astype(BF16)
        acc[0, i, half:count] = mine(u, -1, half, rest)
        prevs[u] = net.push(acc.at[0, i, pl.ds(0, count)], f_next.at[i, pl.ds(0, count)], net.dev(first, -1))
        lows[u].wait_recv()
        acc[1, i, half:count] = (mine(u, 1, half, rest).astype(F32) + q_low[i, :rest].astype(F32)).astype(BF16)
        acc[1, i, :half] = mine(u, 1, 0, half)
        nexts[u] = net.push(acc.at[1, i, pl.ds(0, count)], f_prev.at[i, pl.ds(0, count)], net.dev(first, 1))
    yield

    def total(i, u):
        prevs[u].wait_recv()
        nexts[u].wait_recv()
        return mine(u, 0, 0, count).astype(F32) + f_next[i, :count].astype(F32) + f_prev[i, :count].astype(F32)

    acc[2, 0, :count] = total(0, 2).astype(BF16)
    top = net.push(acc.at[2, 0, pl.ds(0, half)], q_top.at[4, pl.ds(0, half)], net.dev(second, -1))
    bot = net.push(acc.at[2, 0, pl.ds(half, rest)], q_low.at[4, pl.ds(0, rest)], net.dev(second, 1))
    yield
    t = total(1, -1)
    top.wait_recv()
    acc[2, 1, :half] = (t[:half] + q_top[4, :half].astype(F32)).astype(BF16)
    acc[2, 1, half:count] = t[half:].astype(BF16)
    prev = net.push(acc.at[2, 1, pl.ds(0, count)], f_next.at[4, pl.ds(0, count)], net.dev(second, -1))
    t = total(2, 1)
    bot.wait_recv()
    acc[2, 2, half:count] = (t[half:] + q_low[4, :rest].astype(F32)).astype(BF16)
    acc[2, 2, :half] = t[:half].astype(BF16)
    nxt = net.push(acc.at[2, 2, pl.ds(0, count)], f_prev.at[4, pl.ds(0, count)], net.dev(second, 1))
    yield
    t = total(3, 0)
    prev.wait_recv()
    nxt.wait_recv()
    out[low:low + count] = t + f_next[4, :count].astype(F32) + f_prev[4, :count].astype(F32)


def scatter_row(net, src, sib, q_top, q_low, f_next, f_prev, out):
    half = 256
    orders = (2, -1, 1, 0)

    def at(dx, k):
        return src.at[lax.rem(net.x + dx + 4, 4) * 2 + k]

    pair = [net.push(at(u, 1 - net.k), sib.at[i], net.dev("k")) for i, u in enumerate(orders)]

    def own(u):
        return src[lax.rem(net.x + u + 4, 4) * 2 + net.k]

    yield
    pair[0].wait_recv()
    sib[0] = sib[0] + own(2)
    top = net.push(sib.at[0, pl.ds(0, half)], q_top, net.dev("x", -1))
    low = net.push(sib.at[0, pl.ds(half, half)], q_low, net.dev("x", 1))
    yield
    pair[1].wait_recv()
    sib[1] = sib[1] + own(-1)
    top.wait_recv()
    sib[1, :half] = sib[1, :half] + q_top[...]
    prev = net.push(sib.at[1], f_next, net.dev("x", -1))
    pair[2].wait_recv()
    sib[2] = sib[2] + own(1)
    low.wait_recv()
    sib[2, half:] = sib[2, half:] + q_low[...]
    nxt = net.push(sib.at[2], f_prev, net.dev("x", 1))
    yield
    pair[3].wait_recv()
    t = sib[3] + own(0)
    yield
    prev.wait_recv()
    nxt.wait_recv()
    out[...] = t + f_next[...] + f_prev[...]


PLANE_SCRATCH = [pltpu.VMEM((3, 4, 224, WIDTH), BF16), pltpu.VMEM((5, 112, WIDTH), BF16),
                 pltpu.VMEM((5, 112, WIDTH), BF16), pltpu.VMEM((5, 224, WIDTH), BF16),
                 pltpu.VMEM((5, 224, WIDTH), BF16)]


def row_scratch(n):
    return [pltpu.VMEM((4, 512, n), F32), pltpu.VMEM((256, n), F32), pltpu.VMEM((256, n), F32),
            pltpu.VMEM((512, n), F32), pltpu.VMEM((512, n), F32)]


def scatter_kernel(mix, ngrad, wo, wq, wkv, gain, inner, mix_out, ngrad_out, wo_out, wq_out, wkv_out,
                   gain_out, inner_out, *rest):
    planes = [rest[5 * i:5 * i + 5] for i in range(4)]
    rows = [rest[20 + 5 * i:25 + 5 * i] for i in range(3)]
    gains, inners, gain_sum, gain_rows, send, recv = rest[35:]
    net = Net(send, recv)
    others = [(net.r, lax.rem(net.c + d, 16)) for d in range(1, 16)]
    peers = [(lax.rem(net.r + d, 8), net.c) for d in range(1, 8)]
    net.greet(others + peers)
    small = []
    for d, dev in enumerate(others):
        small.append(net.push(gain.at[lax.rem(net.c + d + 1, 16)], gains.at[d], dev))
        small.append(net.push(inner, inners.at[d], dev))

    def little():
        yield
        yield
        for copy in small:
            copy.wait_recv()
        g, n = gain[net.c], inner[...]
        for d in range(15):
            g = g + gains[d]
            n = n + inners[d]
        inner_out[...] = n
        gain_sum[...] = g
        final = [net.push(gain_sum, gain_rows.at[d], dev) for d, dev in enumerate(peers)]
        yield
        yield
        for copy in final:
            copy.wait_recv()
        for d in range(7):
            g = g + gain_rows[d]
        gain_out[...] = g

    run([
        scatter_row(net, wo, *rows[0], wo_out),
        scatter_plane(net, mix, *planes[0], 0, 224, 112, "y", mix_out),
        scatter_plane(net, mix, *planes[1], 224, 224, 112, "z", mix_out),
        scatter_row(net, wq, *rows[1], wq_out),
        scatter_plane(net, ngrad, *planes[2], 0, 224, 112, "y", ngrad_out),
        scatter_plane(net, ngrad, *planes[3], 224, 224, 112, "z", ngrad_out),
        scatter_row(net, wkv, *rows[2], wkv_out),
        little(),
    ])
    net.finish()


def scatter_all(mix, ngrad, wo, wq, wkv, gain, inner):
    copies = 30 + 7 + 4 * 20 + 3 * 8
    return pl.pallas_call(
        scatter_kernel,
        out_shape=(
            jax.ShapeDtypeStruct((BLOCK, WIDTH), F32), jax.ShapeDtypeStruct((BLOCK, WIDTH), F32),
            jax.ShapeDtypeStruct((512, 256), F32), jax.ShapeDtypeStruct((512, 256), F32),
            jax.ShapeDtypeStruct((512, 128), F32), jax.ShapeDtypeStruct((8, WIDTH), F32),
            jax.ShapeDtypeStruct((8, 128), F32),
        ),
        in_specs=[VM] * 7,
        out_specs=(VM,) * 7,
        scratch_shapes=PLANE_SCRATCH * 4 + row_scratch(256) * 2 + row_scratch(128) + [
            pltpu.VMEM((15, 8, WIDTH), F32), pltpu.VMEM((15, 8, 128), F32), pltpu.VMEM((8, WIDTH), F32),
            pltpu.VMEM((7, 8, WIDTH), F32),
            pltpu.SemaphoreType.DMA((copies,)), pltpu.SemaphoreType.DMA((copies,))],
        compiler_params=pltpu.CompilerParams(collective_id=5, has_side_effects=True, vmem_limit_bytes=VMEM_MOST),
        name="scatter_all",
    )(mix, ngrad, wo, wq, wkv, gain, inner)


def body(tokens, norm_gain, w_query, w_key, w_value, w_out, out_grad, doc_lengths):
    row, col = lax.axis_index("row"), lax.axis_index("col")
    extra = jnp.broadcast_to(norm_gain[None, :], (EXTRA, WIDTH))
    tok3, grad3, wqkv, wo3 = gather_all(
        jnp.concatenate([tokens, extra], axis=0), out_grad, w_query, w_key, w_value, w_out)
    wqkv = wqkv.reshape(4096, 512)

    ends = jnp.cumsum(doc_lengths)
    spots = jnp.arange(8 * BLOCK, dtype=jnp.int32)
    before = spots[:, None] >= ends[None, :]
    starts = jnp.sum(jnp.where(before, doc_lengths[None, :], 0), axis=1)
    first = row * BLOCK
    last = first + BLOCK - 1
    low = jnp.sum(jnp.where(first >= ends, doc_lengths, 0)) // TILE
    high = jnp.sum(doc_lengths * (jnp.concatenate([jnp.zeros((1,), ends.dtype), ends[:-1]]) <= last))
    bounds = jnp.stack([row, low, (last + TILE) // TILE - low, first // TILE,
                        (high + TILE - 1) // TILE - first // TILE]).astype(jnp.int32)
    own_starts = lax.dynamic_slice_in_dim(starts, first, BLOCK, 0)[:, None]
    row_starts = jnp.broadcast_to(starts[None, :], (8, 8 * BLOCK))

    normed3, pack, inverse = project(tok3, grad3, wqkv, wo3)
    packs = share(pack).reshape(8 * BLOCK, 768)
    attended, d_query, stats = query_side(bounds, own_starts, packs)
    all_stats = share_stats(stats[:, :8].T)
    all_stats = all_stats.transpose(1, 0, 2).reshape(8, 8 * BLOCK)
    d_kv = key_side(bounds, row_starts, all_stats, packs)

    side = lax.rem(col, 2)
    halves = d_kv.reshape(BLOCK, 4, 2, 64)
    keep = lax.dynamic_index_in_dim(halves, side, 2, keepdims=False)
    give = lax.dynamic_index_in_dim(halves, 1 - side, 2, keepdims=False)
    got = swap_pair(give.reshape(BLOCK, 256)).reshape(BLOCK, 4, 64)
    four = keep.astype(F32) + got.astype(F32)
    four = jnp.concatenate([four[:, 0] + four[:, 1], four[:, 2] + four[:, 3]], axis=1)
    upper = lax.reduce_precision(four, 8, 7)
    both = jnp.concatenate([upper, four - upper], axis=1).astype(BF16)

    mix, ngrad, gain, inner = parts(attended, d_query, d_kv, inverse, tok3, wqkv, wo3)
    wq_terms = jnp.einsum("ctd,tn->cdn", normed3, d_query, preferred_element_type=F32).reshape(8, 512, 256)
    kv_terms = jnp.einsum("ctd,tn->cdn", normed3, both, preferred_element_type=F32)
    kv_terms = (kv_terms[:, :, :128] + kv_terms[:, :, 128:]).reshape(8, 512, 128)
    wo_terms = jnp.einsum("ti,ctd->cid", attended, grad3, preferred_element_type=F32).reshape(8, 512, 256)
    inner = jnp.pad(jnp.sum(inner, axis=1), (0, 1024 - BLOCK)).reshape(8, 128)
    mixed, ngrad, wo_grad, wq_grad, kv_grad, gain_grad, inner = scatter_all(
        mix, ngrad, wo_terms, wq_terms, kv_terms, gain, inner)

    own_tokens = tokens.astype(F32)
    layer_out = (own_tokens + mixed).astype(BF16)
    inner_mean = inner.reshape(1024)[:BLOCK, None] * (1.0 / 4096)
    scaled_grad = ngrad * norm_gain.astype(F32)[None, :]
    token_grad = out_grad.astype(F32) + inverse * scaled_grad - own_tokens * inverse**3 * inner_mean
    out_weight_grad = wo_grad.reshape(2, 256, 256).transpose(1, 0, 2).reshape(256, 512)
    return (layer_out, token_grad, jnp.sum(gain_grad, axis=0), wq_grad,
            kv_grad[:, :64], kv_grad[:, 64:], out_weight_grad)


def solution(mesh):
    in_specs = (P("row", "col"), P("col"), P("row", "col"), P("row", None), P("row", None),
                P("col", "row"), P("row", "col"), P())
    out_specs = (P("row", "col"), P("row", "col"), P("col"), P("row", "col"), P("row", "col"),
                 P("row", "col"), P("col", "row"))
    return jax.shard_map(body, mesh=mesh, in_specs=in_specs, out_specs=out_specs, check_vma=False)
```

```python
import functools

import jax
import jax.numpy as jnp
from jax import lax
from jax.experimental import pallas as pl
from jax.experimental.pallas import tpu as pltpu
from jax.sharding import PartitionSpec as P

HEAD_DIM = 128
BLOCK = 448
EXTRA = 16
WIDTH = 256
TILE = 256
MOST_TILES = 10
eps = 1e-05
FACTOR = HEAD_DIM ** (-0.5)
F32 = jnp.float32
BF16 = jnp.bfloat16
ANY = pl.BlockSpec(memory_space=pl.ANY)
VM = pl.BlockSpec(memory_space=pltpu.VMEM)
VMEM_MOST = 60 * 1024 * 1024


class Net:
    def __init__(self, send, recv):
        self.send, self.recv, self.used, self.open = send, recv, 0, []
        self.r, self.c = lax.axis_index("row"), lax.axis_index("col")
        self.x, self.k = self.r // 2, lax.rem(self.r, 2)
        self.y, self.z = self.c // 4, lax.rem(self.c, 4)

    def dev(self, axis, step=1):
        if axis == "k":
            return (self.x * 2 + 1 - self.k, self.c)
        if axis == "x":
            return (lax.rem(self.x + step + 4, 4) * 2 + self.k, self.c)
        if axis == "y":
            return (self.r, self.col(step, 0))
        return (self.r, self.col(0, step))

    def col(self, dy, dz):
        return lax.rem(self.y + dy + 4, 4) * 4 + lax.rem(self.z + dz + 4, 4)

    def greet(self, devices):
        bar = pltpu.get_barrier_semaphore()
        for d in devices:
            pl.semaphore_signal(bar, inc=1, device_id=d, device_id_type=pl.DeviceIdType.MESH)
        pl.semaphore_wait(bar, len(devices))

    def push(self, src, dst, device):
        i = self.used
        self.used += 1
        copy = pltpu.make_async_remote_copy(
            src_ref=src, dst_ref=dst, send_sem=self.send.at[i], recv_sem=self.recv.at[i],
            device_id=device, device_id_type=pl.DeviceIdType.MESH)
        copy.start()
        self.open.append(copy)
        return copy

    def finish(self):
        for copy in self.open:
            copy.wait_send()


def run(streams):
    streams = list(streams)
    while streams:
        left = []
        for s in streams:
            try:
                next(s)
                left.append(s)
            except StopIteration:
                pass
        streams = left


def gather_plane(net, own, at, low, count, half, first):
    second = "z" if first == "y" else "y"

    def blk(da, db, lo=low, n=count):
        dy, dz = (da, db) if first == "y" else (db, da)
        return at(net.col(dy, dz), lo, n)

    t0, tn = low, half
    b0, bn = low + half, count - half
    mine = own(low, count)
    ar = net.push(mine, blk(0, 0), net.dev(first, 1))
    al = net.push(mine, blk(0, 0), net.dev(first, -1))
    br = {0: net.push(mine, blk(0, 0), net.dev(second, 1))}
    bl = {0: net.push(mine, blk(0, 0), net.dev(second, -1))}
    tail = []

    def send_unit(u):
        br[u] = net.push(blk(u, 0), blk(u, 0), net.dev(second, 1))
        bl[u] = net.push(blk(u, 0), blk(u, 0), net.dev(second, -1))

    def relay_unit(u):
        br[u].wait_recv()
        tail.append(net.push(blk(u, -1, t0, tn), blk(u, -1, t0, tn), net.dev(second, 1)))
        bl[u].wait_recv()
        tail.append(net.push(blk(u, 1, b0, bn), blk(u, 1, b0, bn), net.dev(second, -1)))

    yield
    ar.wait_recv()
    fr = net.push(blk(-1, 0, t0, tn), blk(-1, 0, t0, tn), net.dev(first, 1))
    send_unit(-1)
    al.wait_recv()
    fl = net.push(blk(1, 0, b0, bn), blk(1, 0, b0, bn), net.dev(first, -1))
    send_unit(1)
    yield
    relay_unit(0)
    yield
    fr.wait_recv()
    fl.wait_recv()
    send_unit(2)
    yield
    relay_unit(-1)
    relay_unit(1)
    yield
    relay_unit(2)
    yield
    for copy in tail:
        copy.wait_recv()


def gather_row(net, parts, at, half):
    sent = [[net.push(s, d, net.dev(a, e)) for s, d in parts] for a, e in (("x", 1), ("x", -1), ("k", 1))]

    def blk(dx, lo=0, n=None):
        return at(lax.rem(net.x + dx + 4, 4) * 2 + net.k, lo, n)

    yield
    for c in sent[0]:
        c.wait_recv()
    fr = net.push(blk(-1, 0, half), blk(-1, 0, half), net.dev("x", 1))
    tail = [net.push(blk(-1), blk(-1), net.dev("k"))]
    for c in sent[1]:
        c.wait_recv()
    fl = net.push(blk(1, half, half), blk(1, half, half), net.dev("x", -1))
    tail.append(net.push(blk(1), blk(1), net.dev("k")))
    yield
    yield
    fr.wait_recv()
    tail.append(net.push(blk(2, 0, half), blk(2, 0, half), net.dev("k")))
    fl.wait_recv()
    tail.append(net.push(blk(2, half, half), blk(2, half, half), net.dev("k")))
    yield
    yield
    for c in sent[2] + tail:
        c.wait_recv()


def load(moves, sems):
    copies = [pltpu.make_async_copy(src, dst, sems.at[i]) for i, (src, dst) in enumerate(moves)]
    for copy in copies:
        copy.start()
    return copies


def later(n, stream):
    for _ in range(n):
        yield
    yield from stream


def first_kernel(tok, row_gain, grad, wq, wk, wv, wo,
                 tok_out, grad_out, wqkv_out, wo_out, norm_out, kv_out, q_out, g_out, inverse,
                 tok3, grad3, wqkv, wo3, norm_t, kv, qs, gs, sums, inv, qkv, gsum, send, recv, here, away):
    net = Net(send, recv)
    r, c = net.r, net.c
    slot = pl.multiple_of(c // 2 * HEAD_DIM, HEAD_DIM)
    wk_own, wv_own = wk.at[:, pl.ds(slot, HEAD_DIM)], wv.at[:, pl.ds(slot, HEAD_DIM)]
    q_at, k_at, v_at = (wqkv.at[r, :, pl.ds(0, 256)], wqkv.at[r, :, pl.ds(256, 128)],
                        wqkv.at[r, :, pl.ds(384, 128)])

    def at3(ref):
        return lambda i, lo, n: ref.at[i, pl.ds(lo, n)]

    def whole(ref, rows):
        return lambda i, lo, n: ref.at[i, pl.ds(lo, rows if n is None else n)]

    def own(ref):
        return lambda lo, n: ref.at[pl.ds(lo, n)]

    ins = load([(tok, tok3.at[c, pl.ds(0, BLOCK)]), (wq, q_at), (wk_own, k_at), (wv_own, v_at),
                (grad, grad3.at[c]), (wo, wo3.at[r])], here)
    tok3[c, BLOCK:BLOCK + EXTRA, :] = jnp.broadcast_to(row_gain[...], (EXTRA, WIDTH))
    net.greet([net.dev("y", 1), net.dev("y", -1), net.dev("z", 1), net.dev("z", -1),
               net.dev("x", 1), net.dev("x", -1), net.dev("k")])
    ins[0].wait()
    tokens = [
        gather_plane(net, own(tok3.at[c]), at3(tok3), 0, 224, 112, "y"),
        gather_plane(net, own(tok3.at[c]), at3(tok3), 224, 240, 112, "z"),
        gather_row(net, [(wq, q_at), (wk_own, k_at), (wv_own, v_at)], whole(wqkv, 512), 256),
    ]
    grads = [
        gather_row(net, [(wo, wo3.at[r])], whole(wo3, 256), 128),
        gather_plane(net, own(grad), at3(grad3), 0, 224, 112, "y"),
        gather_plane(net, own(grad), at3(grad3), 224, 224, 112, "z"),
    ]
    outs = []

    def keep(src, dst):
        copy = pltpu.make_async_copy(src, dst, away.at[len(outs)])
        copy.start()
        outs.append(copy)

    def step(streams):
        for s in list(streams):
            try:
                next(s)
            except StopIteration:
                streams.remove(s)

    step(tokens)
    step(tokens)
    step(grads)
    while tokens:
        step(tokens)
        if len(tokens) > 0:
            step(grads)
    for copy in ins[1:]:
        copy.wait()

    sums[...] = jnp.zeros_like(sums)

    @pl.loop(0, 16)
    def _(i):
        t = tok3[i, :BLOCK, :].astype(F32)
        sums[...] += fold(t * t)

    scale = lax.rsqrt(jnp.sum(sums[...], axis=1, keepdims=True) * (1.0 / 4096) + eps)
    inverse[...] = scale
    inv[...] = jnp.broadcast_to(scale, inv.shape)
    qkv[...] = jnp.zeros_like(qkv)

    @pl.loop(0, 8)
    def _(i):
        both = []
        for j in range(2):
            t = tok3[2 * i + j, :BLOCK, :].astype(F32) * jnp.concatenate([inv[...], inv[...]], axis=1)
            n = (t * tok3[2 * i + j, BLOCK:BLOCK + 1, :].astype(F32)).astype(BF16)
            norm_t[2 * i + j] = n.T
            both.append(n)
        qkv[...] += jnp.dot(jnp.concatenate(both, axis=1), wqkv[i], preferred_element_type=F32)

    kv[r] = qkv[:, 256:].astype(BF16)
    qs[r] = qkv[:, :256].astype(BF16)
    shares = [gather_row(net, [(ref.at[r], ref.at[r])], whole(ref, BLOCK), 224) for ref in (kv, qs)]
    step(shares)
    keep(tok3, tok_out)
    keep(norm_t, norm_out)
    while grads:
        step(grads)
        step(shares)
    keep(grad3, grad_out)
    keep(wqkv, wqkv_out)
    keep(wo3, wo_out)
    gsum[...] = jnp.zeros_like(gsum)

    @pl.loop(0, 8)
    def _(i):
        gsum[...] += (lax.dot_general(grad3[2 * i], wo3[i, :, :256], NT, preferred_element_type=F32)
                      + lax.dot_general(grad3[2 * i + 1], wo3[i, :, 256:], NT, preferred_element_type=F32))

    gs[r] = gsum[...].astype(BF16)
    last = gather_row(net, [(gs.at[r], gs.at[r])], whole(gs, BLOCK), 224)
    next(last)
    while shares:
        step(shares)
    keep(kv, kv_out)
    keep(qs, q_out)
    run([last])
    keep(gs, g_out)
    for o in outs:
        o.wait()
    net.finish()


def first_part(tok, row_gain, grad, wq, wk, wv, wo):
    rows = BLOCK + EXTRA
    copies = 2 * 2 * 20 + 15 + 4 * 9
    big = [((16, rows, WIDTH), BF16), ((16, BLOCK, WIDTH), BF16), ((8, 512, 512), BF16), ((8, 256, 512), BF16),
           ((16, WIDTH, BLOCK), BF16)] + [((8, BLOCK, 256), BF16)] * 3
    return pl.pallas_call(
        first_kernel,
        out_shape=[jax.ShapeDtypeStruct(*b) for b in big] + [jax.ShapeDtypeStruct((BLOCK, 1), F32)],
        in_specs=[ANY, VM] + [ANY] * 5,
        out_specs=[ANY] * 8 + [VM],
        scratch_shapes=[pltpu.VMEM(*b) for b in big] + [
            pltpu.VMEM((BLOCK, 128), F32), pltpu.VMEM((BLOCK, 128), F32), pltpu.VMEM((BLOCK, 512), F32),
            pltpu.VMEM((BLOCK, 256), F32),
            pltpu.SemaphoreType.DMA((copies,)), pltpu.SemaphoreType.DMA((copies,)),
            pltpu.SemaphoreType.DMA((6,)), pltpu.SemaphoreType.DMA((8,)),
        ],
        compiler_params=pltpu.CompilerParams(collective_id=1, has_side_effects=True, vmem_limit_bytes=VMEM_MOST),
        name="first_part",
    )(tok, row_gain, grad, wq, wk, wv, wo)


NT = (((1,), (1,)), ((), ()))


def fold(a):
    return a[:, :128] + a[:, 128:]


def doc_start(spot, docs):
    start, end = jnp.zeros_like(spot), 0
    for d in range(4):
        end = end + docs[d]
        start = jnp.where(spot >= end, end, start)
    return start


def doc_bounds(docs, first):
    low, high, end = 0, 0, 0
    for d in range(4):
        high = jnp.where(first + BLOCK - 1 >= end, end + docs[d], high)
        end = end + docs[d]
        low = jnp.where(first >= end, end, low)
    return low, high


def query_kernel(docs, qs, gs, kv, att, att_t, dq, stats, s_all, dp_all, m_part, l_part, w_part, a_sum, q_sum):
    r = lax.axis_index("row")
    base = r * BLOCK
    low = doc_bounds(docs, base)[0] // TILE
    count = (base + BLOCK + TILE - 1) // TILE - low
    spot = base + lax.broadcasted_iota(jnp.int32, (BLOCK, 1), 0)
    first = doc_start(spot, docs)
    lane = lax.broadcasted_iota(jnp.int32, (BLOCK, 128), 1)
    table = jnp.zeros((BLOCK, 128), F32)
    for h in range(2):
        q = qs[pl.ds(pl.multiple_of(base, 64), BLOCK), h * 128:(h + 1) * 128]
        g = gs[pl.ds(pl.multiple_of(base, 64), BLOCK), h * 128:(h + 1) * 128]
        m_part[...] = jnp.full_like(m_part, -1e30)
        l_part[...] = jnp.zeros_like(l_part)
        w_part[...] = jnp.zeros_like(w_part)
        a_sum[...] = jnp.zeros_like(a_sum)
        q_sum[...] = jnp.zeros_like(q_sum)

        def rows(i):
            return pl.ds(pl.multiple_of((low + i) * TILE, TILE), TILE)

        @pl.loop(0, count)
        def _(i):
            s = lax.dot_general(q, kv[rows(i), :128], NT, preferred_element_type=F32) * FACTOR
            key = (low + i) * TILE + lax.broadcasted_iota(jnp.int32, (1, TILE), 1)
            s = jnp.where((key <= spot) & (key >= first), s, -1e30)
            s_all[i] = s
            m_part[...] = jnp.maximum(m_part[...], jnp.maximum(s[:, :128], s[:, 128:]))

        m = jnp.max(m_part[...], axis=1, keepdims=True)

        @pl.loop(0, count)
        def _(i):
            e = jnp.exp(s_all[i] - m)
            dp = lax.dot_general(g, kv[rows(i), 128:], NT, preferred_element_type=F32)
            s_all[i] = e
            dp_all[i] = dp
            l_part[...] += fold(e)
            w_part[...] += fold(e * dp)

        inv = 1.0 / jnp.sum(l_part[...], axis=1, keepdims=True)
        w = jnp.sum(w_part[...], axis=1, keepdims=True) * inv

        @pl.loop(0, count)
        def _(i):
            p = s_all[i] * inv
            d = (p * (dp_all[i] - w) * FACTOR).astype(BF16)
            a_sum[...] += jnp.dot(p.astype(BF16), kv[rows(i), 128:], preferred_element_type=F32)
            q_sum[...] += jnp.dot(d, kv[rows(i), :128], preferred_element_type=F32)

        att[:, h * 128:(h + 1) * 128] = a_sum[...].astype(BF16)
        att_t[h * 128:(h + 1) * 128, :] = a_sum[...].T.astype(BF16)
        dq[:, h * 128:(h + 1) * 128] = q_sum[...].astype(BF16)
        for j, v in enumerate((m, inv, w)):
            table = jnp.where(lane == 3 * h + j, v, table)
    stats[...] = table.T[:8, :]


SMEM = pl.BlockSpec(memory_space=pltpu.SMEM)


def query_side(docs, qs, gs, kv):
    return pl.pallas_call(
        query_kernel,
        out_shape=(jax.ShapeDtypeStruct((BLOCK, 256), BF16), jax.ShapeDtypeStruct((256, BLOCK), BF16),
                   jax.ShapeDtypeStruct((BLOCK, 256), BF16), jax.ShapeDtypeStruct((8, BLOCK), F32)),
        in_specs=[SMEM, VM, VM, VM],
        out_specs=(VM,) * 4,
        scratch_shapes=[pltpu.VMEM((MOST_TILES, BLOCK, TILE), F32)] * 2 + [pltpu.VMEM((BLOCK, 128), F32)] * 5,
        compiler_params=pltpu.CompilerParams(vmem_limit_bytes=VMEM_MOST),
        name="query_side",
    )(docs, qs, gs, kv)


def key_kernel(docs, stats, qs, gs, kv, out, keep, give, k_sum, v_sum, k_two, v_two):
    r = lax.axis_index("row")
    base = r * BLOCK
    low = base // TILE
    count = (doc_bounds(docs, base)[1] + TILE - 1) // TILE - low
    key = base + lax.broadcasted_iota(jnp.int32, (BLOCK, 1), 0)
    k = kv[pl.ds(pl.multiple_of(base, 64), BLOCK), :128]
    v = kv[pl.ds(pl.multiple_of(base, 64), BLOCK), 128:]
    for h in range(2):
        k_sum[...] = jnp.zeros_like(k_sum)
        v_sum[...] = jnp.zeros_like(v_sum)

        @pl.loop(0, count)
        def _(i):
            at = pl.ds(pl.multiple_of((low + i) * TILE, TILE), TILE)
            q = qs[at, h * 128:(h + 1) * 128]
            g = gs[at, h * 128:(h + 1) * 128]
            m, inv, w = (stats[3 * h + j:3 * h + j + 1, at] for j in range(3))
            spot = (low + i) * TILE + lax.broadcasted_iota(jnp.int32, (1, TILE), 1)
            s = lax.dot_general(k, q, NT, preferred_element_type=F32) * FACTOR
            s = jnp.where((key <= spot) & (key >= doc_start(spot, docs)), s, -1e30)
            p = jnp.exp(s - m) * inv
            dp = lax.dot_general(v, g, NT, preferred_element_type=F32)
            d = (p * (dp - w) * FACTOR).astype(BF16)
            v_sum[...] += jnp.dot(p.astype(BF16), g, preferred_element_type=F32)
            k_sum[...] += jnp.dot(d, q, preferred_element_type=F32)

        for total, two in ((k_sum, k_two), (v_sum, v_two)):
            d = total[...].astype(BF16).astype(F32)
            two[...] = d if h == 0 else two[...] + d

    even = lax.rem(lax.axis_index("col"), 2) == 0
    k, v = k_two[...], v_two[...]
    for j, two in enumerate((k, v)):
        upper = two.astype(BF16)
        out[:, j * 128:(j + 1) * 128] = upper
        out[:, 256 + j * 128:256 + (j + 1) * 128] = (two - upper.astype(F32)).astype(BF16)
    left = jnp.concatenate([k[:, :64], v[:, :64]], axis=1)
    right = jnp.concatenate([k[:, 64:], v[:, 64:]], axis=1)
    keep[...] = jnp.where(even, left, right)
    give[...] = jnp.where(even, right, left)


def key_side(docs, stats, qs, gs, kv):
    return pl.pallas_call(
        key_kernel,
        out_shape=(jax.ShapeDtypeStruct((BLOCK, 512), BF16), jax.ShapeDtypeStruct((BLOCK, 128), F32),
                   jax.ShapeDtypeStruct((BLOCK, 128), F32)),
        in_specs=[SMEM, VM, VM, VM, VM],
        out_specs=(VM,) * 3,
        scratch_shapes=[pltpu.VMEM((BLOCK, 128), F32)] * 4,
        compiler_params=pltpu.CompilerParams(vmem_limit_bytes=VMEM_MOST),
        name="key_side",
    )(docs, stats, qs, gs, kv)


def stats_kernel(own, out, send, recv, here):
    net = Net(send, recv)
    peers = [(lax.rem(net.r + d, 8), net.c) for d in range(1, 8)]
    net.greet(peers)
    copies = [net.push(own, out.at[net.r], p) for p in peers]
    local = pltpu.make_async_copy(own, out.at[net.r], here.at[0])
    local.start()
    for copy in copies:
        copy.wait_recv()
    local.wait()
    net.finish()


def share_stats(own):
    return pl.pallas_call(
        stats_kernel,
        out_shape=jax.ShapeDtypeStruct((8, 8, BLOCK), F32),
        in_specs=[VM],
        out_specs=VM,
        scratch_shapes=[pltpu.SemaphoreType.DMA((7,)), pltpu.SemaphoreType.DMA((7,)),
                        pltpu.SemaphoreType.DMA((1,))],
        compiler_params=pltpu.CompilerParams(collective_id=3, has_side_effects=True),
        name="share_stats",
    )(own)


def scatter_plane(net, src, acc, q_top, q_low, f_next, f_prev, low, count, half, first, out):
    second = "z" if first == "y" else "y"

    def mine(da, db, lo, n):
        dy, dz = (db, da) if first == "y" else (da, db)
        return src[net.col(dy, dz), pl.ds(low + lo, n), :]

    def mine_at(da, db, lo, n):
        dy, dz = (db, da) if first == "y" else (da, db)
        return src.at[net.col(dy, dz), pl.ds(low + lo, n)]

    rest = count - half
    units = (2, -1, 1, 0)
    tops, lows, nexts, prevs = {}, {}, {}, {}
    for i, u in enumerate(units):
        tops[u] = net.push(mine_at(u, 2, 0, half), q_top.at[i, pl.ds(0, half)], net.dev(first, -1))
        lows[u] = net.push(mine_at(u, 2, half, rest), q_low.at[i, pl.ds(0, rest)], net.dev(first, 1))
    yield
    for i, u in enumerate(units):
        tops[u].wait_recv()
        acc[0, i, :half] = (mine(u, -1, 0, half).astype(F32) + q_top[i, :half].astype(F32)).astype(BF16)
        acc[0, i, half:count] = mine(u, -1, half, rest)
        prevs[u] = net.push(acc.at[0, i, pl.ds(0, count)], f_next.at[i, pl.ds(0, count)], net.dev(first, -1))
        lows[u].wait_recv()
        acc[1, i, half:count] = (mine(u, 1, half, rest).astype(F32) + q_low[i, :rest].astype(F32)).astype(BF16)
        acc[1, i, :half] = mine(u, 1, 0, half)
        nexts[u] = net.push(acc.at[1, i, pl.ds(0, count)], f_prev.at[i, pl.ds(0, count)], net.dev(first, 1))
    yield

    def total(i, u):
        prevs[u].wait_recv()
        nexts[u].wait_recv()
        return mine(u, 0, 0, count).astype(F32) + f_next[i, :count].astype(F32) + f_prev[i, :count].astype(F32)

    acc[2, 0, :count] = total(0, 2).astype(BF16)
    top = net.push(acc.at[2, 0, pl.ds(0, half)], q_top.at[4, pl.ds(0, half)], net.dev(second, -1))
    bot = net.push(acc.at[2, 0, pl.ds(half, rest)], q_low.at[4, pl.ds(0, rest)], net.dev(second, 1))
    yield
    t = total(1, -1)
    top.wait_recv()
    acc[2, 1, :half] = (t[:half] + q_top[4, :half].astype(F32)).astype(BF16)
    acc[2, 1, half:count] = t[half:].astype(BF16)
    prev = net.push(acc.at[2, 1, pl.ds(0, count)], f_next.at[4, pl.ds(0, count)], net.dev(second, -1))
    t = total(2, 1)
    bot.wait_recv()
    acc[2, 2, half:count] = (t[half:] + q_low[4, :rest].astype(F32)).astype(BF16)
    acc[2, 2, :half] = t[:half].astype(BF16)
    nxt = net.push(acc.at[2, 2, pl.ds(0, count)], f_prev.at[4, pl.ds(0, count)], net.dev(second, 1))
    yield
    t = total(3, 0)
    prev.wait_recv()
    nxt.wait_recv()
    out(low, count, t + f_next[4, :count].astype(F32) + f_prev[4, :count].astype(F32))


def scatter_row(net, src, sib, q_top, q_low, f_next, f_prev, out):
    half = src.shape[1] // 2
    orders = (2, -1, 1, 0)

    def at(dx, k):
        return src.at[lax.rem(net.x + dx + 4, 4) * 2 + k]

    pair = [net.push(at(u, 1 - net.k), sib.at[i], net.dev("k")) for i, u in enumerate(orders)]

    def own(u):
        return src[lax.rem(net.x + u + 4, 4) * 2 + net.k]

    yield
    pair[0].wait_recv()
    sib[0] = sib[0] + own(2)
    top = net.push(sib.at[0, pl.ds(0, half)], q_top, net.dev("x", -1))
    low = net.push(sib.at[0, pl.ds(half, half)], q_low, net.dev("x", 1))
    yield
    pair[1].wait_recv()
    sib[1] = sib[1] + own(-1)
    top.wait_recv()
    sib[1, :half] = sib[1, :half] + q_top[...]
    prev = net.push(sib.at[1], f_next, net.dev("x", -1))
    pair[2].wait_recv()
    sib[2] = sib[2] + own(1)
    low.wait_recv()
    sib[2, half:] = sib[2, half:] + q_low[...]
    nxt = net.push(sib.at[2], f_prev, net.dev("x", 1))
    yield
    pair[3].wait_recv()
    sib[3] = sib[3] + own(0)
    yield
    yield
    prev.wait_recv()
    nxt.wait_recv()
    out(sib[3] + f_next[...] + f_prev[...])


PLANE_SCRATCH = [pltpu.VMEM((3, 4, 224, WIDTH), BF16), pltpu.VMEM((5, 112, WIDTH), BF16),
                 pltpu.VMEM((5, 112, WIDTH), BF16), pltpu.VMEM((5, 224, WIDTH), BF16),
                 pltpu.VMEM((5, 224, WIDTH), BF16)]


def row_scratch(m, n):
    return [pltpu.VMEM((8, m, n), F32), pltpu.VMEM((4, m, n), F32), pltpu.VMEM((m // 2, n), F32),
            pltpu.VMEM((m // 2, n), F32), pltpu.VMEM((m, n), F32), pltpu.VMEM((m, n), F32)]


def last_kernel(att_in, att_t_in, dq_in, dkv_in, keep_in, give, inv_in, tok_in, grad_in, wqkv_in, wo_in, norm_in,
                layer_out, token_grad, gain_grad, wq_grad, wk_grad, wv_grad, wo_grad,
                att, att_t, dq, dkv, keep, inverse, tok3, grad3, wqkv, wo3, norm_t, mix, ngrad, got, both,
                gain, inner_sum, inner, gains, inners, gain_all, gain_rows, *rest):
    planes = [rest[5 * i:5 * i + 5] for i in range(4)]
    wo_terms, wq_terms, kv_terms = (rest[20 + 6 * i:26 + 6 * i] for i in range(3))
    send, recv, here = rest[38:]
    ins = load([(att_in, att), (wo_in, wo3), (att_t_in, att_t), (grad_in, grad3), (dq_in, dq), (norm_in, norm_t),
                (dkv_in, dkv), (wqkv_in, wqkv), (tok_in, tok3), (inv_in, inverse), (keep_in, keep)], here)
    net = Net(send, recv)
    others = [(net.r, lax.rem(net.c + d, 16)) for d in range(1, 16)]
    peers = [(lax.rem(net.r + d, 8), net.c) for d in range(1, 8)]
    net.greet(others + peers)
    swap = net.push(give, got, (net.r, net.c + 1 - 2 * lax.rem(net.c, 2)))
    live = []

    def step():
        for s in list(live):
            try:
                next(s)
            except StopIteration:
                live.remove(s)

    def start(*streams):
        for s in streams:
            next(s)
            live.append(s)

    def put_layer(lo, n, total):
        layer_out[lo:lo + n] = (tok3[net.c, lo:lo + n, :].astype(F32) + total).astype(BF16)

    def put_grad(lo, n, total):
        token_grad[lo:lo + n] = total

    def put(ref):
        def write(total):
            ref[...] = total
        return write

    def put_kv(total):
        flat = total.T
        wk_grad[...] = flat[:64]
        wv_grad[...] = flat[64:]

    for copy in ins[:2]:
        copy.wait()

    @pl.loop(0, 8)
    def _(i):
        mix[2 * i] = jnp.dot(att[...], wo3[i, :, :256], preferred_element_type=F32).astype(BF16)
        mix[2 * i + 1] = jnp.dot(att[...], wo3[i, :, 256:], preferred_element_type=F32).astype(BF16)

    start(scatter_plane(net, mix, *planes[0], 0, 224, 112, "y", put_layer),
          scatter_plane(net, mix, *planes[1], 224, 224, 112, "z", put_layer))
    for copy in ins[2:4]:
        copy.wait()

    @pl.loop(0, 8)
    def _(i):
        wo_terms[0][i, :, :256] = jnp.dot(att_t[...], grad3[2 * i], preferred_element_type=F32)
        wo_terms[0][i, :, 256:] = jnp.dot(att_t[...], grad3[2 * i + 1], preferred_element_type=F32)

    start(scatter_row(net, *wo_terms, put(wo_grad)))
    for copy in ins[4:6]:
        copy.wait()

    @pl.loop(0, 8)
    def _(i):
        wq_terms[0][i, :256] = jnp.dot(norm_t[2 * i], dq[...], preferred_element_type=F32)
        wq_terms[0][i, 256:] = jnp.dot(norm_t[2 * i + 1], dq[...], preferred_element_type=F32)

    step()
    start(scatter_row(net, *wq_terms, put(wq_grad)))
    for copy in ins[6:]:
        copy.wait()
    inner_sum[...] = jnp.zeros_like(inner_sum)
    for part in range(4):

        @pl.loop(2 * part, 2 * part + 2)
        def _(i):
            for j in range(2):
                at = pl.ds(j * 256, 256)
                g = lax.dot_general(dq[...], wqkv[i, at, :256], NT, preferred_element_type=F32)
                for h in range(2):
                    g += lax.dot_general(dkv[:, h * 256:(h + 1) * 256], wqkv[i, at, 256:], NT,
                                         preferred_element_type=F32)
                ngrad[2 * i + j] = g.astype(BF16)
                a = g * tok3[2 * i + j, :BLOCK, :].astype(F32)
                inner_sum[...] += fold(a * tok3[2 * i + j, BLOCK:BLOCK + 1, :].astype(F32))
                gain[2 * i + j] = jnp.sum((a * inverse[...]).reshape(BLOCK // 8, 8, WIDTH), axis=0)

        step()

    start(scatter_plane(net, ngrad, *planes[2], 0, 224, 112, "y", put_grad),
          scatter_plane(net, ngrad, *planes[3], 224, 224, 112, "z", put_grad))
    inner[...] = jnp.broadcast_to(jnp.sum(inner_sum[...].T, axis=0, keepdims=True), inner.shape)
    small = []
    for d, dev in enumerate(others):
        small.append(net.push(gain.at[lax.rem(net.c + d + 1, 16)], gains.at[d], dev))
        small.append(net.push(inner, inners.at[d], dev))
    swap.wait_recv()
    four = keep[...] + got[...]
    upper = four.astype(BF16)
    both[:, :128] = upper
    both[:, 128:] = (four - upper.astype(F32)).astype(BF16)

    @pl.loop(0, 8)
    def _(i):
        for j in range(2):
            t = jnp.dot(norm_t[2 * i + j], both[...], preferred_element_type=F32)
            kv_terms[0][i, j * 256:(j + 1) * 256] = fold(t)

    start(scatter_row(net, *kv_terms, put_kv))
    step()
    for copy in small:
        copy.wait_recv()
    g, total = gain[net.c], inner[...]
    for d in range(15):
        g = g + gains[d]
        total = total + inners[d]
    gain_all[...] = g
    final = [net.push(gain_all, gain_rows.at[d], dev) for d, dev in enumerate(peers)]
    while live:
        step()
    for copy in final:
        copy.wait_recv()
    for d in range(7):
        g = g + gain_rows[d]
    gain_grad[...] = jnp.sum(g, axis=0, keepdims=True)
    mean = jnp.broadcast_to(total[0:1], (128, BLOCK)).T * (1.0 / 4096)
    i = inverse[...]
    scaled = token_grad[...] * tok3[net.c, BLOCK:BLOCK + 1, :].astype(F32)
    token_grad[...] = (grad3[net.c].astype(F32) + i * scaled
                       - tok3[net.c, :BLOCK, :].astype(F32) * i**3 * jnp.concatenate([mean, mean], axis=1))
    net.finish()


def last_part(*operands):
    rows = operands[7].shape[1]
    copies = 1 + 30 + 7 + 4 * 20 + 3 * 8
    return pl.pallas_call(
        last_kernel,
        out_shape=[
            jax.ShapeDtypeStruct((BLOCK, WIDTH), BF16), jax.ShapeDtypeStruct((BLOCK, WIDTH), F32),
            jax.ShapeDtypeStruct((1, WIDTH), F32), jax.ShapeDtypeStruct((512, 256), F32),
            jax.ShapeDtypeStruct((64, 512), F32), jax.ShapeDtypeStruct((64, 512), F32),
            jax.ShapeDtypeStruct((256, 512), F32),
        ],
        in_specs=[ANY] * 12,
        out_specs=[VM] * 7,
        scratch_shapes=[
            pltpu.VMEM((BLOCK, 256), BF16), pltpu.VMEM((256, BLOCK), BF16), pltpu.VMEM((BLOCK, 256), BF16),
            pltpu.VMEM((BLOCK, 512), BF16), pltpu.VMEM((BLOCK, 128), F32), pltpu.VMEM((BLOCK, 1), F32),
            pltpu.VMEM((16, rows, WIDTH), BF16), pltpu.VMEM((16, BLOCK, WIDTH), BF16),
            pltpu.VMEM((8, 512, 512), BF16), pltpu.VMEM((8, 256, 512), BF16), pltpu.VMEM((16, WIDTH, BLOCK), BF16),
            pltpu.VMEM((16, BLOCK, WIDTH), BF16), pltpu.VMEM((16, BLOCK, WIDTH), BF16),
            pltpu.VMEM((BLOCK, 128), F32), pltpu.VMEM((BLOCK, 256), BF16),
            pltpu.VMEM((16, 8, WIDTH), F32), pltpu.VMEM((BLOCK, 128), F32), pltpu.VMEM((8, BLOCK), F32),
            pltpu.VMEM((15, 8, WIDTH), F32), pltpu.VMEM((15, 8, BLOCK), F32), pltpu.VMEM((8, WIDTH), F32),
            pltpu.VMEM((7, 8, WIDTH), F32),
        ] + PLANE_SCRATCH * 4 + row_scratch(256, 512) + row_scratch(512, 256) + row_scratch(512, 128) + [
            pltpu.SemaphoreType.DMA((copies,)), pltpu.SemaphoreType.DMA((copies,)), pltpu.SemaphoreType.DMA((11,))],
        compiler_params=pltpu.CompilerParams(collective_id=5, has_side_effects=True,
                                             vmem_limit_bytes=63 * 1024 * 1024),
        name="last_part",
    )(*operands)


def hand_kernel(*refs):
    for src, dst in zip(refs[:7], refs[7:]):
        dst[...] = src[...]


def hand_over(*arrays):
    return pl.pallas_call(
        hand_kernel,
        out_shape=[jax.ShapeDtypeStruct(a.shape, a.dtype) for a in arrays],
        in_specs=[VM] * 7,
        out_specs=[VM] * 7,
        name="hand_over",
    )(*arrays)


def body(tokens, norm_gain, w_query, w_key, w_value, w_out, out_grad, doc_lengths):
    tok3, grad3, wqkv, wo3, norm_t, kv, qs, gs, inverse = first_part(
        tokens, norm_gain.reshape(1, WIDTH), out_grad, w_query, w_key, w_value, w_out)
    qs, gs, kv = (a.reshape(8 * BLOCK, 256) for a in (qs, gs, kv))
    attended, attended_t, d_query, stats = query_side(doc_lengths, qs, gs, kv)
    all_stats = share_stats(stats).transpose(1, 0, 2).reshape(8, 8 * BLOCK)
    d_kv, keep, give = key_side(doc_lengths, all_stats, qs, gs, kv)
    layer_out, token_grad, gain_grad, wq_grad, wk_grad, wv_grad, wo_grad = hand_over(*last_part(
        attended, attended_t, d_query, d_kv, keep, give, inverse, tok3, grad3, wqkv, wo3, norm_t))
    return layer_out, token_grad, gain_grad.reshape(WIDTH), wq_grad, wk_grad.T, wv_grad.T, wo_grad


def solution(mesh):
    in_specs = (P("row", "col"), P("col"), P("row", "col"), P("row", None), P("row", None),
                P("col", "row"), P("row", "col"), P())
    out_specs = (P("row", "col"), P("row", "col"), P("col"), P("row", "col"), P("row", "col"),
                 P("row", "col"), P("col", "row"))
    return jax.shard_map(body, mesh=mesh, in_specs=in_specs, out_specs=out_specs, check_vma=False)
```

```python
import functools

import jax
import jax.numpy as jnp
from jax import lax
from jax.experimental import pallas as pl
from jax.experimental.pallas import tpu as pltpu
from jax.sharding import PartitionSpec as P

HEAD_DIM = 128
BLOCK = 448
EXTRA = 16
WIDTH = 256
TILE = 256
MOST_TILES = 10
eps = 1e-05
FACTOR = HEAD_DIM ** (-0.5)
F32 = jnp.float32
BF16 = jnp.bfloat16
ANY = pl.BlockSpec(memory_space=pl.ANY)
SMEM = pl.BlockSpec(memory_space=pltpu.SMEM)
VM = pl.BlockSpec(memory_space=pltpu.VMEM)
VMEM_MOST = 67043328
NT = (((1,), (1,)), ((), ()))


class Net:
    def __init__(self, send, recv):
        self.send, self.recv, self.used, self.open = send, recv, 0, []
        self.r, self.c = lax.axis_index("row"), lax.axis_index("col")
        self.x, self.k = self.r // 2, lax.rem(self.r, 2)
        self.y, self.z = self.c // 4, lax.rem(self.c, 4)

    def dev(self, axis, step=1):
        if axis == "k":
            return (self.x * 2 + 1 - self.k, self.c)
        if axis == "x":
            return (lax.rem(self.x + step + 4, 4) * 2 + self.k, self.c)
        if axis == "y":
            return (self.r, self.col(step, 0))
        return (self.r, self.col(0, step))

    def col(self, dy, dz):
        return lax.rem(self.y + dy + 4, 4) * 4 + lax.rem(self.z + dz + 4, 4)

    def greet(self, devices):
        bar = pltpu.get_barrier_semaphore()
        for d in devices:
            pl.semaphore_signal(bar, inc=1, device_id=d, device_id_type=pl.DeviceIdType.MESH)
        pl.semaphore_wait(bar, len(devices))

    def push(self, src, dst, device):
        i = self.used
        self.used += 1
        copy = pltpu.make_async_remote_copy(
            src_ref=src, dst_ref=dst, send_sem=self.send.at[i], recv_sem=self.recv.at[i],
            device_id=device, device_id_type=pl.DeviceIdType.MESH)
        copy.start()
        self.open.append(copy)
        return copy

    def finish(self, count=None):
        for copy in self.open[:count]:
            copy.wait_send()
        self.open = [] if count is None else self.open[count:]


def gather_plane(net, at, low, count, half, first):
    second = "z" if first == "y" else "y"
    top, bot = (low, half), (low + half, count - half)
    rest = []

    def blk(da, db, rows):
        dy, dz = (da, db) if first == "y" else (db, da)
        return at(net.col(dy, dz), *rows)

    def push(da, db, rows, axis, way):
        copy = net.push(blk(da, db, rows), blk(da, db, rows), net.dev(axis, way))
        rest.append(copy)
        return copy

    def recv(copy):
        rest[:] = [other for other in rest if other is not copy]
        copy.wait_recv()

    a_next, a_prev = push(0, 0, top, first, 1), push(0, 0, bot, first, -1)
    nexts, prevs = {0: push(0, 0, top, second, 1)}, {0: push(0, 0, bot, second, -1)}
    a_next2, a_prev2 = push(0, 0, bot, first, 1), push(0, 0, top, first, -1)
    push(0, 0, bot, second, 1)
    push(0, 0, top, second, -1)

    def relay(u):
        recv(nexts[u])
        push(u, -1, top, second, 1)
        recv(prevs[u])
        push(u, 1, bot, second, -1)

    yield
    recv(a_next)
    f_next = push(-1, 0, top, first, 1)
    nexts[-1] = push(-1, 0, top, second, 1)
    recv(a_prev)
    f_prev = push(1, 0, bot, first, -1)
    prevs[1] = push(1, 0, bot, second, -1)
    relay(0)
    yield
    recv(a_next2)
    prevs[-1] = push(-1, 0, bot, second, -1)
    push(-1, 0, bot, second, 1)
    push(-1, 0, top, second, -1)
    recv(a_prev2)
    nexts[1] = push(1, 0, top, second, 1)
    push(1, 0, bot, second, 1)
    push(1, 0, top, second, -1)
    yield
    recv(f_next)
    nexts[2] = push(2, 0, top, second, 1)
    recv(f_prev)
    prevs[2] = push(2, 0, bot, second, -1)
    push(2, 0, bot, second, 1)
    push(2, 0, top, second, -1)
    yield
    relay(-1)
    relay(1)
    yield
    relay(2)
    yield
    for copy in rest:
        copy.wait_recv()


def gather_row(net, parts, at, half):
    def send(way, lo):
        return [net.push(s.at[pl.ds(lo, half)], d.at[pl.ds(lo, half)], net.dev("x", way)) for s, d in parts]

    def blk(dx, lo=0, n=None):
        return at(lax.rem(net.x + dx + 4, 4) * 2 + net.k, lo, n)

    def push(dx, device, lo=0, n=None):
        return net.push(blk(dx, lo, n), blk(dx, lo, n), device)

    def recv(copies):
        for c in copies:
            c.wait_recv()

    sent = [send(1, 0), send(-1, half), send(1, half), send(-1, 0)]
    tail = [net.push(s, d, net.dev("k")) for s, d in parts]
    yield
    recv(sent[0])
    f_next = push(-1, net.dev("x", 1), 0, half)
    recv(sent[1])
    f_prev = push(1, net.dev("x", -1), half, half)
    yield
    recv(sent[2])
    tail.append(push(-1, net.dev("k")))
    recv(sent[3])
    tail.append(push(1, net.dev("k")))
    yield
    f_next.wait_recv()
    tail.append(push(2, net.dev("k"), 0, half))
    f_prev.wait_recv()
    tail.append(push(2, net.dev("k"), half, half))
    yield
    recv(tail)


def scatter_plane(net, src, q_top, q_low, f_next, f_prev, low, half, first, out):
    second = "z" if first == "y" else "y"
    units = (2, -1, 1, 0)
    t, b = pl.ds(0, half), pl.ds(half, half)

    def col(da, db):
        dy, dz = (db, da) if first == "y" else (da, db)
        return net.col(dy, dz)

    def at(da, db, lo):
        return src.at[col(da, db), pl.ds(low + lo, half)]

    def add(da, db, lo, value):
        rows = slice(low + lo, low + lo + half)
        i = col(da, db)
        src[i, rows, :] = (src[i, rows, :].astype(F32) + value.astype(F32)).astype(BF16)

    tops, lows, waits = {}, {}, {}
    for i, u in enumerate(units):
        tops[u] = net.push(at(u, 2, 0), q_top.at[i], net.dev(first, -1))
        lows[u] = net.push(at(u, 2, half), q_low.at[i], net.dev(first, 1))
    for i, u in enumerate(units):
        waits[u] = [net.push(at(u, -1, half), f_next.at[i, b], net.dev(first, -1)),
                    net.push(at(u, 1, 0), f_prev.at[i, t], net.dev(first, 1))]
    yield
    for i, u in enumerate(units):
        tops[u].wait_recv()
        add(u, -1, 0, q_top[i])
        waits[u].append(net.push(at(u, -1, 0), f_next.at[i, t], net.dev(first, -1)))
        lows[u].wait_recv()
        add(u, 1, half, q_low[i])
        waits[u].append(net.push(at(u, 1, half), f_prev.at[i, b], net.dev(first, 1)))
    yield

    def total(i, u):
        for copy in waits[u]:
            copy.wait_recv()
        rows = slice(low, low + 2 * half)
        return src[col(u, 0), rows, :].astype(F32) + f_next[i].astype(F32) + f_prev[i].astype(F32)

    def settle(i, u):
        value = total(i, u).astype(BF16)
        src[col(u, 0), low:low + 2 * half, :] = value

    settle(0, 2)
    top = net.push(at(2, 0, 0), q_top.at[4], net.dev(second, -1))
    bot = net.push(at(2, 0, half), q_low.at[4], net.dev(second, 1))
    settle(1, -1)
    final = [net.push(at(-1, 0, half), f_next.at[4, b], net.dev(second, -1))]
    settle(2, 1)
    final.append(net.push(at(1, 0, 0), f_prev.at[4, t], net.dev(second, 1)))
    yield
    top.wait_recv()
    add(-1, 0, 0, q_top[4])
    final.append(net.push(at(-1, 0, 0), f_next.at[4, t], net.dev(second, -1)))
    bot.wait_recv()
    add(1, 0, half, q_low[4])
    final.append(net.push(at(1, 0, half), f_prev.at[4, b], net.dev(second, 1)))
    yield
    last = total(3, 0)
    for copy in final:
        copy.wait_recv()
    out(low, 2 * half, last + f_next[4].astype(F32) + f_prev[4].astype(F32))


def scatter_row(net, at, sib, far, q_top, q_low, f_next, f_prev, out):
    half = 256
    t, b = pl.ds(0, half), pl.ds(half, half)

    def block(dx, k):
        return at(lax.rem(net.x + dx + 4, 4), k)

    pair = [net.push(block(u, 1 - net.k), sib.at[i], net.dev("k")) for i, u in enumerate((2, -1, 1, 0))]

    def join(i, u):
        pair[i].wait_recv()
        sib[i] = sib[i] + block(u, net.k)[...]

    yield
    join(0, 2)
    far[...] = sib[0].astype(BF16)
    top = net.push(far.at[t], q_top, net.dev("x", -1))
    low = net.push(far.at[b], q_low, net.dev("x", 1))
    join(1, -1)
    final = [net.push(sib.at[1, b], f_next.at[b], net.dev("x", -1))]
    join(2, 1)
    final.append(net.push(sib.at[2, t], f_prev.at[t], net.dev("x", 1)))
    yield
    top.wait_recv()
    sib[1, :half] = sib[1, :half] + q_top[...].astype(F32)
    final.append(net.push(sib.at[1, t], f_next.at[t], net.dev("x", -1)))
    low.wait_recv()
    sib[2, half:] = sib[2, half:] + q_low[...].astype(F32)
    final.append(net.push(sib.at[2, b], f_prev.at[b], net.dev("x", 1)))
    yield
    join(3, 0)
    yield
    for copy in final:
        copy.wait_recv()
    sib[3] = sib[3] + f_next[...] + f_prev[...]
    out(sib.at[3])


PLANE_SCRATCH = [((5, 112, WIDTH), BF16), ((5, 112, WIDTH), BF16), ((5, 224, WIDTH), BF16), ((5, 224, WIDTH), BF16)]


def row_scratch(n):
    return [((4, 512, n), F32), ((512, n), BF16), ((256, n), BF16), ((256, n), BF16), ((512, n), F32),
            ((512, n), F32)]


def doc_start(spot, docs):
    start, end = jnp.zeros_like(spot), 0
    for d in range(4):
        end = end + docs[d]
        start = jnp.where(spot >= end, end, start)
    return start


def fold(a):
    return a[:, :128] + a[:, 128:]


def whole_kernel(docs, tok, row_gain, grad, wq, wk, wv, wo,
                 layer_out, token_grad, gain_grad, wq_grad, wk_grad, wv_grad, wo_grad,
                 tok3, grad3, wqkv, wo3, norm_t, kv, qs, gs, big, mix, own_grad, part_a, part_b, inv, qkv, dkv,
                 att, att_t, dq, keep, give, got, own_stats, stats, gain, inner, gains, inners, gain_all, gain_rows,
                 *rest):
    planes = [rest[4 * i:4 * i + 4] for i in range(4)]
    rows = [rest[16 + 6 * i:22 + 6 * i] for i in range(3)]
    send, recv, here, away = rest[34:]
    net = Net(send, recv)
    r, c = net.r, net.c
    slot = pl.multiple_of(c // 2 * HEAD_DIM, HEAD_DIM)
    wk_own, wv_own = wk.at[:, pl.ds(slot, HEAD_DIM)], wv.at[:, pl.ds(slot, HEAD_DIM)]
    q_at, k_at, v_at = (wqkv.at[r, :, pl.ds(0, 256)], wqkv.at[r, :, pl.ds(256, 128)],
                        wqkv.at[r, :, pl.ds(384, 128)])
    others = [(r, lax.rem(c + d, 16)) for d in range(1, 16)]
    peers = [(lax.rem(r + d, 8), c) for d in range(1, 8)]
    live = []

    def step(some=None):
        for s in list(live):
            if some is None or s in some:
                try:
                    next(s)
                except StopIteration:
                    live.remove(s)

    def start(*streams):
        for s in streams:
            next(s)
            live.append(s)

    def at3(ref):
        return lambda i, lo, n: ref.at[i, pl.ds(lo, n)]

    def whole(ref, m):
        return lambda i, lo, n: ref.at[i, pl.ds(lo, m if n is None else n)]

    ins = []
    for i, (src, dst) in enumerate([
            (tok, tok3.at[c, pl.ds(0, BLOCK)]), (grad, grad3.at[c]), (wq, q_at), (wk_own, k_at), (wv_own, v_at),
            (wo, wo3.at[r])]):
        ins.append(pltpu.make_async_copy(src, dst, here.at[i]))
        ins[-1].start()
    tok3[c, BLOCK:BLOCK + EXTRA, :] = jnp.broadcast_to(row_gain[...], (EXTRA, WIDTH))
    net.greet(others + peers)
    ins[0].wait()
    tokens = (gather_plane(net, at3(tok3), 0, 224, 112, "y"), gather_plane(net, at3(tok3), 224, 240, 112, "z"))
    w_share = gather_row(net, [(wq, q_at), (wk_own, k_at), (wv_own, v_at)], whole(wqkv, 512), 256)
    grads = (gather_plane(net, at3(grad3), 0, 224, 112, "y"), gather_plane(net, at3(grad3), 224, 224, 112, "z"))
    o_share = gather_row(net, [(wo, wo3.at[r])], whole(wo3, 256), 128)
    start(*tokens, w_share)
    for copy in ins[1:]:
        copy.wait()
    for some in (tokens, tokens, (w_share,), tokens, tokens, (w_share,)):
        step(some)
    start(*grads, o_share)
    for some in (tokens, (w_share,), tokens, grads, (w_share,)):
        step(some)

    part_a[...] = jnp.zeros_like(part_a)

    @pl.loop(0, 16)
    def _(i):
        t = tok3[i, :BLOCK, :].astype(F32)
        part_a[...] += fold(t * t)

    step(grads)
    scale = lax.rsqrt(jnp.sum(part_a[...], axis=1, keepdims=True) * (1.0 / 4096) + eps)
    inv[...] = jnp.broadcast_to(scale, inv.shape)
    qkv[...] = jnp.zeros_like(qkv)

    for piece in range(2):

        @pl.loop(4 * piece, 4 * piece + 4)
        def _(i):
            both = []
            for j in range(2):
                t = tok3[2 * i + j, :BLOCK, :].astype(F32) * jnp.concatenate([inv[...], inv[...]], axis=1)
                n = (t * tok3[2 * i + j, BLOCK:BLOCK + 1, :].astype(F32)).astype(BF16)
                norm_t[2 * i + j] = n.T
                both.append(n)
            qkv[...] += jnp.dot(jnp.concatenate(both, axis=1), wqkv[i], preferred_element_type=F32)

        step(grads)

    kv[r] = qkv[:, 256:].astype(BF16)
    qs[r] = qkv[:, :256].astype(BF16)
    kv_share = gather_row(net, [(kv.at[r], kv.at[r])], whole(kv, BLOCK), 224)
    q_share = gather_row(net, [(qs.at[r], qs.at[r])], whole(qs, BLOCK), 224)
    start(kv_share)
    step(grads)
    step((o_share,))
    step(grads)
    step((o_share,))
    step((kv_share,))
    while any(g in live for g in grads):
        step(grads)
    step((kv_share,))
    while o_share in live:
        step((o_share,))

    part = qkv.at[:, pl.ds(0, 256)]
    part[...] = jnp.zeros((BLOCK, 256), F32)

    @pl.loop(0, 8)
    def _(i):
        part[...] += (lax.dot_general(grad3[2 * i], wo3[i, :, :256], NT, preferred_element_type=F32)
                      + lax.dot_general(grad3[2 * i + 1], wo3[i, :, 256:], NT, preferred_element_type=F32))

    gs[r] = qkv[:, :256].astype(BF16)
    gathered = len(net.open)
    g_share = gather_row(net, [(gs.at[r], gs.at[r])], whole(gs, BLOCK), 224)
    start(g_share, q_share)
    while kv_share in live:
        step((kv_share,))

    base = r * BLOCK
    low = jnp.maximum(r - 4, 0) * BLOCK // TILE
    count = (base + BLOCK + TILE - 1) // TILE - low
    spot = base + lax.broadcasted_iota(jnp.int32, (BLOCK, 1), 0)
    first = doc_start(spot, docs)
    lane = lax.broadcasted_iota(jnp.int32, (BLOCK, 128), 1)
    table = jnp.zeros((BLOCK, 128), F32)
    kept = []

    def keys(i):
        return pl.ds(pl.multiple_of((low + i) * TILE, TILE), TILE)

    def slot_of(h, i):
        return pl.ds(pl.multiple_of((10 * h + i) * BLOCK, 64), BLOCK)

    def lot(base, i, m=512):
        return pl.ds(pl.multiple_of(base + i * m, 256), m)

    flat = kv.reshape(8 * BLOCK, 256)
    for h in range(2):
        q = qs[r, :, h * 128:(h + 1) * 128]
        part_a[...] = jnp.full_like(part_a, -1e30)

        @pl.loop(0, count)
        def _(i):
            s = lax.dot_general(q, flat[keys(i), :128], NT, preferred_element_type=F32) * FACTOR
            key = (low + i) * TILE + lax.broadcasted_iota(jnp.int32, (1, TILE), 1)
            s = jnp.where((key <= spot) & (key >= first), s, -1e30)
            big[slot_of(h, i), :] = s
            part_a[...] = jnp.maximum(part_a[...], jnp.maximum(s[:, :128], s[:, 128:]))

        m = jnp.max(part_a[...], axis=1, keepdims=True)
        part_a[...] = jnp.zeros_like(part_a)

        @pl.loop(0, count)
        def _(i):
            e = jnp.exp(big[slot_of(h, i), :] - m)
            big[slot_of(h, i), :] = e
            part_a[...] += fold(e)

        over = 1.0 / jnp.sum(part_a[...], axis=1, keepdims=True)
        part_a[...] = jnp.zeros_like(part_a)

        @pl.loop(0, count)
        def _(i):
            p = (big[slot_of(h, i), :] * over).astype(BF16)
            part_a[...] += jnp.dot(p, flat[keys(i), 128:], preferred_element_type=F32)

        att[:, h * 128:(h + 1) * 128] = part_a[...].astype(BF16)
        att_t[h * 128:(h + 1) * 128, :] = part_a[...].T.astype(BF16)
        kept.append((m, over))
        step((g_share, q_share))

    def put_layer(lo, n, total):
        layer_out[lo:lo + n] = (tok3[c, lo:lo + n, :].astype(F32) + total).astype(BF16)

    def put_grad(lo, n, total):
        token_grad[lo:lo + n] = total

    outs = []

    def put_out(src, dst):
        outs.append(pltpu.make_async_copy(src, dst, away.at[len(outs)]))
        outs[-1].start()

    def put_wo(total):
        put_out(total.at[pl.ds(0, 256)], wo_grad.at[:, pl.ds(0, 256)])
        put_out(total.at[pl.ds(256, 256)], wo_grad.at[:, pl.ds(256, 256)])

    def put_wq(total):
        put_out(total, wq_grad)

    def put_kv(total):
        side = total[...].T
        wk_grad[...] = side[:64]
        wv_grad[...] = side[64:]

    @pl.loop(0, 8)
    def _(i):
        mix[2 * i] = jnp.dot(att[...], wo3[i, :, :256], preferred_element_type=F32).astype(BF16)
        mix[2 * i + 1] = jnp.dot(att[...], wo3[i, :, 256:], preferred_element_type=F32).astype(BF16)

    mixes = (scatter_plane(net, mix, *planes[0], 0, 112, "y", put_layer),
             scatter_plane(net, mix, *planes[1], 224, 112, "z", put_layer))
    start(*mixes)

    @pl.loop(0, 16)
    def _(i):
        big[lot(20 * BLOCK, i, 256), :] = jnp.dot(att_t[...], grad3[i], preferred_element_type=F32)

    wo_sum = scatter_row(net, lambda x, k: big.at[lot(20 * BLOCK, 2 * x + k)], *rows[0], put_wo)
    start(wo_sum)

    for h in range(2):
        m, over = kept[h]
        g = gs[r, :, h * 128:(h + 1) * 128]
        part_a[...] = jnp.zeros_like(part_a)
        part_b[...] = jnp.zeros_like(part_b)

        @pl.loop(0, count)
        def _(i):
            dp = lax.dot_general(g, flat[keys(i), 128:], NT, preferred_element_type=F32)
            part_a[...] += fold(big[slot_of(h, i), :] * dp)

        w = jnp.sum(part_a[...], axis=1, keepdims=True) * over

        @pl.loop(0, count)
        def _(i):
            dp = lax.dot_general(g, flat[keys(i), 128:], NT, preferred_element_type=F32)
            d = (big[slot_of(h, i), :] * over * (dp - w) * FACTOR).astype(BF16)
            part_b[...] += jnp.dot(d, flat[keys(i), :128], preferred_element_type=F32)

        dq[:, h * 128:(h + 1) * 128] = part_b[...].astype(BF16)
        for j, v in enumerate((m, over, w)):
            table = jnp.where(lane == 3 * h + j, v, table)
        step((g_share, q_share))
        if h == 0:
            step((wo_sum,))
            step(mixes)
    own_stats[...] = table.T[:8, :]
    told = [net.push(own_stats, stats.at[r], p) for p in peers]
    stats[r] = own_stats[...]

    @pl.loop(0, 16)
    def _(i):
        big[lot(0, i, 256), :] = jnp.dot(norm_t[i], dq[...], preferred_element_type=F32)

    wq_sum = scatter_row(net, lambda x, k: big.at[lot(0, 2 * x + k)], *rows[1], put_wq)
    start(wq_sum)
    step((wo_sum,))
    while q_share in live or g_share in live:
        step((q_share, g_share))
    for copy in told:
        copy.wait_recv()

    key = base + lax.broadcasted_iota(jnp.int32, (BLOCK, 1), 0)
    k, v = kv[r, :, :128], kv[r, :, 128:]
    sums = [(ref, at) for at in (0, 128) for ref in (qkv.at[:, pl.ds(at, 128)], qkv.at[:, pl.ds(256 + at, 128)])]
    qkv[...] = jnp.zeros_like(qkv)
    for b in range(5):

        @pl.when(r + b < 8)
        def _():
            o = r + b
            row = o * BLOCK + lax.broadcasted_iota(jnp.int32, (1, BLOCK), 1)
            seen = (key <= row) & (key >= doc_start(row, docs))
            for h in range(2):
                cols = slice(h * 128, (h + 1) * 128)
                more = slice(256 + h * 128, 256 + (h + 1) * 128)
                q, g = qs[o, :, cols], gs[o, :, cols]
                m, over, w = (stats[o, 3 * h + j:3 * h + j + 1, :] for j in range(3))
                s = lax.dot_general(k, q, NT, preferred_element_type=F32) * FACTOR
                p = jnp.exp(jnp.where(seen, s, -1e30) - m) * over
                dp = lax.dot_general(v, g, NT, preferred_element_type=F32)
                d = (p * (dp - w) * FACTOR).astype(BF16)
                qkv[:, more] += jnp.dot(p.astype(BF16), g, preferred_element_type=F32)
                qkv[:, cols] += jnp.dot(d, q, preferred_element_type=F32)

        if b == 0:
            step(mixes)
        if b == 2:
            step((wq_sum,))
        if b == 3:
            step(mixes)

    two = [qkv[:, at:at + 128].astype(BF16).astype(F32) + qkv[:, at + 128:at + 256].astype(BF16).astype(F32)
           for at in (0, 256)]
    for j, value in enumerate(two):
        upper = value.astype(BF16)
        dkv[:, j * 128:(j + 1) * 128] = upper
        dkv[:, 256 + j * 128:256 + (j + 1) * 128] = (value - upper.astype(F32)).astype(BF16)
    even = lax.rem(c, 2) == 0
    left = jnp.concatenate([two[0][:, :64], two[1][:, :64]], axis=1)
    right = jnp.concatenate([two[0][:, 64:], two[1][:, 64:]], axis=1)
    keep[...] = jnp.where(even, left, right)
    give[...] = jnp.where(even, right, left)
    swap = net.push(give, got, (r, c + 1 - 2 * lax.rem(c, 2)))

    own_grad[...] = grad3[c]
    net.finish(gathered)
    ngrad = grad3
    part_a[...] = jnp.zeros_like(part_a)
    for piece in range(2):

        @pl.loop(4 * piece, 4 * piece + 4)
        def _(i):
            for j in range(2):
                at = pl.ds(j * 256, 256)
                g = lax.dot_general(dq[...], wqkv[i, at, :256], NT, preferred_element_type=F32)
                for h in range(2):
                    g += lax.dot_general(dkv[:, h * 256:(h + 1) * 256], wqkv[i, at, 256:], NT,
                                         preferred_element_type=F32)
                ngrad[2 * i + j] = g.astype(BF16)
                a = g * tok3[2 * i + j, :BLOCK, :].astype(F32)
                part_a[...] += fold(a * tok3[2 * i + j, BLOCK:BLOCK + 1, :].astype(F32))
                a = a * jnp.concatenate([inv[...], inv[...]], axis=1)
                gain[2 * i + j] = jnp.sum(a.reshape(BLOCK // 8, 8, WIDTH), axis=0)

        if piece == 0:
            step(mixes)

    ngs = (scatter_plane(net, ngrad, *planes[2], 0, 112, "y", put_grad),
           scatter_plane(net, ngrad, *planes[3], 224, 112, "z", put_grad))
    start(*ngs)
    inner[...] = jnp.broadcast_to(jnp.sum(part_a[...].T, axis=0, keepdims=True), inner.shape)
    small = []
    for d, dev in enumerate(others):
        small.append(net.push(gain.at[lax.rem(c + d + 1, 16)], gains.at[d], dev))
        small.append(net.push(inner, inners.at[d], dev))
    swap.wait_recv()
    four = keep[...] + got[...]
    upper = four.astype(BF16)
    dkv[:, :128] = upper
    dkv[:, 128:256] = (four - upper.astype(F32)).astype(BF16)

    @pl.loop(0, 4)
    def _(i):
        for j in range(4):
            t = jnp.dot(norm_t[4 * i + j], dkv[:, :256], preferred_element_type=F32)
            rows_at = pl.ds(pl.multiple_of(4096 + (j % 2) * 256 + i * 512, 256), 256)
            big[rows_at, (j // 2) * 128:(j // 2) * 128 + 128] = fold(t)

    kv_sum = scatter_row(net, lambda x, k: big.at[lot(4096, x), pl.ds(pl.multiple_of(k * 128, 128), 128)],
                         *rows[2], put_kv)
    start(kv_sum)
    for some in ((wo_sum,), ngs, (kv_sum,), mixes, ngs, (wq_sum,), ngs):
        step(some)
    for copy in small:
        copy.wait_recv()
    g, total = gain[c], inner[...]
    for d in range(15):
        g = g + gains[d]
        total = total + inners[d]
    gain_all[...] = g
    final = [net.push(gain_all, gain_rows.at[d], dev) for d, dev in enumerate(peers)]
    while live:
        step()
    for copy in final:
        copy.wait_recv()
    for d in range(7):
        g = g + gain_rows[d]
    gain_grad[...] = jnp.sum(g, axis=0, keepdims=True)
    mean = jnp.broadcast_to(total[0:1], (128, BLOCK)).T * (1.0 / 4096)
    mean = jnp.concatenate([mean, mean], axis=1)
    i = jnp.concatenate([inv[...], inv[...]], axis=1)
    scaled = token_grad[...] * tok3[c, BLOCK:BLOCK + 1, :].astype(F32)
    token_grad[...] = own_grad[...].astype(F32) + i * scaled - tok3[c, :BLOCK, :].astype(F32) * i**3 * mean
    for copy in outs:
        copy.wait()
    net.finish()


def whole_layer(*operands):
    copies = 4 * 30 + 21 + 4 * 11 + 7 + 1 + 30 + 7 + 4 * 30 + 3 * 10
    scratch = [
        ((16, BLOCK + EXTRA, WIDTH), BF16), ((16, BLOCK, WIDTH), BF16), ((8, 512, 512), BF16), ((8, 256, 512), BF16),
        ((16, WIDTH, BLOCK), BF16), ((8, BLOCK, 256), BF16), ((8, BLOCK, 256), BF16), ((8, BLOCK, 256), BF16),
        ((20 * BLOCK + 4096, 256), F32), ((16, BLOCK, WIDTH), BF16), ((BLOCK, WIDTH), BF16),
        ((BLOCK, 128), F32), ((BLOCK, 128), F32), ((BLOCK, 128), F32), ((BLOCK, 512), F32), ((BLOCK, 512), BF16),
        ((BLOCK, 256), BF16), ((256, BLOCK), BF16), ((BLOCK, 256), BF16), ((BLOCK, 128), F32), ((BLOCK, 128), F32),
        ((BLOCK, 128), F32), ((8, BLOCK), F32), ((8, 8, BLOCK), F32), ((16, 8, WIDTH), F32), ((8, BLOCK), F32),
        ((15, 8, WIDTH), F32), ((15, 8, BLOCK), F32), ((8, WIDTH), F32), ((7, 8, WIDTH), F32),
    ] + PLANE_SCRATCH * 4 + row_scratch(256) * 2 + row_scratch(128)
    return pl.pallas_call(
        whole_kernel,
        out_shape=[
            jax.ShapeDtypeStruct((BLOCK, WIDTH), BF16), jax.ShapeDtypeStruct((BLOCK, WIDTH), F32),
            jax.ShapeDtypeStruct((1, WIDTH), F32), jax.ShapeDtypeStruct((512, 256), F32),
            jax.ShapeDtypeStruct((64, 512), F32), jax.ShapeDtypeStruct((64, 512), F32),
            jax.ShapeDtypeStruct((256, 512), F32),
        ],
        in_specs=[SMEM, ANY, VM] + [ANY] * 5,
        out_specs=[VM, VM, VM, ANY, VM, VM, ANY],
        scratch_shapes=[pltpu.VMEM(*b) for b in scratch] + [
            pltpu.SemaphoreType.DMA((copies,)), pltpu.SemaphoreType.DMA((copies,)), pltpu.SemaphoreType.DMA((6,)),
            pltpu.SemaphoreType.DMA((3,))],
        compiler_params=pltpu.CompilerParams(collective_id=1, has_side_effects=True, vmem_limit_bytes=VMEM_MOST),
        name="whole_layer",
    )(*operands)


def hand_kernel(*refs):
    for src, dst in zip(refs[:7], refs[7:]):
        dst[...] = src[...]


def hand_over(*arrays):
    return pl.pallas_call(
        hand_kernel,
        out_shape=[jax.ShapeDtypeStruct(a.shape, a.dtype) for a in arrays],
        in_specs=[VM] * 7,
        out_specs=[VM] * 7,
        name="hand_over",
    )(*arrays)


def body(tokens, norm_gain, w_query, w_key, w_value, w_out, out_grad, doc_lengths):
    layer_out, token_grad, gain_grad, wq_grad, wk_grad, wv_grad, wo_grad = hand_over(*whole_layer(
        doc_lengths, tokens, norm_gain.reshape(1, WIDTH), out_grad, w_query, w_key, w_value, w_out))
    return layer_out, token_grad, gain_grad.reshape(WIDTH), wq_grad, wk_grad.T, wv_grad.T, wo_grad


def solution(mesh):
    in_specs = (P("row", "col"), P("col"), P("row", "col"), P("row", None), P("row", None),
                P("col", "row"), P("row", "col"), P())
    out_specs = (P("row", "col"), P("row", "col"), P("col"), P("row", "col"), P("row", "col"),
                 P("row", "col"), P("col", "row"))
    return jax.shard_map(body, mesh=mesh, in_specs=in_specs, out_specs=out_specs, check_vma=False)
```

```python
import functools

import jax
import jax.numpy as jnp
from jax import lax
from jax.experimental import pallas as pl
from jax.experimental.pallas import tpu as pltpu
from jax.sharding import PartitionSpec as P

HEAD_DIM = 128
BLOCK = 448
EXTRA = 16
WIDTH = 256
TILE = 256
MOST_TILES = 10
eps = 1e-05
FACTOR = HEAD_DIM ** (-0.5)
F32 = jnp.float32
BF16 = jnp.bfloat16
ANY = pl.BlockSpec(memory_space=pl.ANY)
SMEM = pl.BlockSpec(memory_space=pltpu.SMEM)
VM = pl.BlockSpec(memory_space=pltpu.VMEM)
VMEM_MOST = 67043328
NT = (((1,), (1,)), ((), ()))


POOL = 100


class Net:
    def __init__(self, send, recv):
        self.send, self.recv, self.used, self.open, self.total = send, recv, 0, [], 0
        self.r, self.c = lax.axis_index("row"), lax.axis_index("col")
        self.x, self.k = self.r // 2, lax.rem(self.r, 2)
        self.y, self.z = self.c // 4, lax.rem(self.c, 4)

    def dev(self, axis, step=1):
        if axis == "k":
            return (self.x * 2 + 1 - self.k, self.c)
        if axis == "x":
            return (lax.rem(self.x + step + 4, 4) * 2 + self.k, self.c)
        if axis == "y":
            return (self.r, self.col(step, 0))
        return (self.r, self.col(0, step))

    def col(self, dy, dz):
        return lax.rem(self.y + dy + 4, 4) * 4 + lax.rem(self.z + dz + 4, 4)

    def greet(self, devices):
        bar = pltpu.get_barrier_semaphore()
        for d in devices:
            pl.semaphore_signal(bar, inc=1, device_id=d, device_id_type=pl.DeviceIdType.MESH)
        pl.semaphore_wait(bar, len(devices))

    def push(self, src, dst, device, slot=None):
        if slot is None:
            slot = self.used
            self.used += 1
        if len(self.open) >= POOL:
            self.open.pop(0)[1].wait_send()
        copy = pltpu.make_async_remote_copy(
            src_ref=src, dst_ref=dst, send_sem=self.send.at[self.total % POOL], recv_sem=self.recv.at[slot],
            device_id=device, device_id_type=pl.DeviceIdType.MESH)
        copy.start()
        self.open.append((self.total, copy))
        self.total += 1
        return copy

    def finish(self, count=None):
        while self.open and (count is None or self.open[0][0] < count):
            self.open.pop(0)[1].wait_send()


class Lane:
    def __init__(self, net, *before):
        self.net, self.mine = net, []
        self.old = [slot for lane in before for slot in lane.mine]

    def __getattr__(self, name):
        return getattr(self.net, name)

    def push(self, src, dst, device):
        slot = self.old.pop(0) if self.old else None
        self.mine.append(self.net.used if slot is None else slot)
        return self.net.push(src, dst, device, slot)


def gather_plane(net, at, low, count, half, first):
    second = "z" if first == "y" else "y"
    top, bot = (low, half), (low + half, count - half)
    rest = []

    def blk(da, db, rows):
        dy, dz = (da, db) if first == "y" else (db, da)
        return at(net.col(dy, dz), *rows)

    def push(da, db, rows, axis, way):
        copy = net.push(blk(da, db, rows), blk(da, db, rows), net.dev(axis, way))
        rest.append(copy)
        return copy

    def recv(copy):
        rest[:] = [other for other in rest if other is not copy]
        copy.wait_recv()

    a_next, a_prev = push(0, 0, top, first, 1), push(0, 0, bot, first, -1)
    nexts, prevs = {0: push(0, 0, top, second, 1)}, {0: push(0, 0, bot, second, -1)}
    a_next2, a_prev2 = push(0, 0, bot, first, 1), push(0, 0, top, first, -1)
    push(0, 0, bot, second, 1)
    push(0, 0, top, second, -1)

    def relay(u):
        recv(nexts[u])
        push(u, -1, top, second, 1)
        recv(prevs[u])
        push(u, 1, bot, second, -1)

    yield
    recv(a_next)
    f_next = push(-1, 0, top, first, 1)
    nexts[-1] = push(-1, 0, top, second, 1)
    recv(a_prev)
    f_prev = push(1, 0, bot, first, -1)
    prevs[1] = push(1, 0, bot, second, -1)
    relay(0)
    yield
    recv(a_next2)
    prevs[-1] = push(-1, 0, bot, second, -1)
    push(-1, 0, bot, second, 1)
    push(-1, 0, top, second, -1)
    recv(a_prev2)
    nexts[1] = push(1, 0, top, second, 1)
    push(1, 0, bot, second, 1)
    push(1, 0, top, second, -1)
    yield
    recv(f_next)
    nexts[2] = push(2, 0, top, second, 1)
    recv(f_prev)
    prevs[2] = push(2, 0, bot, second, -1)
    push(2, 0, bot, second, 1)
    push(2, 0, top, second, -1)
    yield
    relay(-1)
    relay(1)
    yield
    relay(2)
    yield
    for copy in rest:
        copy.wait_recv()


def gather_row(net, parts, at, half):
    def send(way, lo):
        return [net.push(s.at[pl.ds(lo, half)], d.at[pl.ds(lo, half)], net.dev("x", way)) for s, d in parts]

    def blk(dx, lo=0, n=None):
        return at(lax.rem(net.x + dx + 4, 4) * 2 + net.k, lo, n)

    def push(dx, device, lo=0, n=None):
        return net.push(blk(dx, lo, n), blk(dx, lo, n), device)

    def recv(copies):
        for c in copies:
            c.wait_recv()

    sent = [send(1, 0), send(-1, half), send(1, half), send(-1, 0)]
    tail = [net.push(s, d, net.dev("k")) for s, d in parts]
    yield
    recv(sent[0])
    f_next = push(-1, net.dev("x", 1), 0, half)
    recv(sent[1])
    f_prev = push(1, net.dev("x", -1), half, half)
    yield
    recv(sent[2])
    tail.append(push(-1, net.dev("k")))
    recv(sent[3])
    tail.append(push(1, net.dev("k")))
    yield
    f_next.wait_recv()
    tail.append(push(2, net.dev("k"), 0, half))
    f_prev.wait_recv()
    tail.append(push(2, net.dev("k"), half, half))
    yield
    recv(tail)


def scatter_plane(net, src, q_top, q_low, f_next, f_prev, low, half, first, out):
    second = "z" if first == "y" else "y"
    units = (2, -1, 1, 0)
    t, b = pl.ds(0, half), pl.ds(half, half)

    def col(da, db):
        dy, dz = (db, da) if first == "y" else (da, db)
        return net.col(dy, dz)

    def at(da, db, lo):
        return src.at[col(da, db), pl.ds(low + lo, half)]

    def add(da, db, lo, value):
        rows = slice(low + lo, low + lo + half)
        i = col(da, db)
        src[i, rows, :] = (src[i, rows, :].astype(F32) + value.astype(F32)).astype(BF16)

    tops, lows, waits = {}, {}, {}
    for i, u in enumerate(units):
        tops[u] = net.push(at(u, 2, 0), q_top.at[i], net.dev(first, -1))
        lows[u] = net.push(at(u, 2, half), q_low.at[i], net.dev(first, 1))
    for i, u in enumerate(units):
        waits[u] = [net.push(at(u, -1, half), f_next.at[i, b], net.dev(first, -1)),
                    net.push(at(u, 1, 0), f_prev.at[i, t], net.dev(first, 1))]
    yield
    for i, u in enumerate(units):
        tops[u].wait_recv()
        add(u, -1, 0, q_top[i])
        waits[u].append(net.push(at(u, -1, 0), f_next.at[i, t], net.dev(first, -1)))
        lows[u].wait_recv()
        add(u, 1, half, q_low[i])
        waits[u].append(net.push(at(u, 1, half), f_prev.at[i, b], net.dev(first, 1)))
    yield

    def total(i, u):
        for copy in waits[u]:
            copy.wait_recv()
        rows = slice(low, low + 2 * half)
        return src[col(u, 0), rows, :].astype(F32) + f_next[i].astype(F32) + f_prev[i].astype(F32)

    def settle(i, u):
        value = total(i, u).astype(BF16)
        src[col(u, 0), low:low + 2 * half, :] = value

    settle(0, 2)
    top = net.push(at(2, 0, 0), q_top.at[4], net.dev(second, -1))
    bot = net.push(at(2, 0, half), q_low.at[4], net.dev(second, 1))
    settle(1, -1)
    final = [net.push(at(-1, 0, half), f_next.at[4, b], net.dev(second, -1))]
    settle(2, 1)
    final.append(net.push(at(1, 0, 0), f_prev.at[4, t], net.dev(second, 1)))
    yield
    top.wait_recv()
    add(-1, 0, 0, q_top[4])
    final.append(net.push(at(-1, 0, 0), f_next.at[4, t], net.dev(second, -1)))
    bot.wait_recv()
    add(1, 0, half, q_low[4])
    final.append(net.push(at(1, 0, half), f_prev.at[4, b], net.dev(second, 1)))
    yield
    last = total(3, 0)
    for copy in final:
        copy.wait_recv()
    out(low, 2 * half, last + f_next[4].astype(F32) + f_prev[4].astype(F32))


def scatter_row(net, at, sib, far, q_top, q_low, f_next, f_prev, out):
    half = 256
    t, b = pl.ds(0, half), pl.ds(half, half)

    def block(dx, k):
        return at(lax.rem(net.x + dx + 4, 4), k)

    pair = [net.push(block(u, 1 - net.k), sib.at[i], net.dev("k")) for i, u in enumerate((2, -1, 1, 0))]

    def join(i, u):
        pair[i].wait_recv()
        sib[i] = sib[i] + block(u, net.k)[...]

    yield
    join(0, 2)
    far[...] = sib[0].astype(BF16)
    top = net.push(far.at[t], q_top, net.dev("x", -1))
    low = net.push(far.at[b], q_low, net.dev("x", 1))
    join(1, -1)
    final = [net.push(sib.at[1, b], f_next.at[b], net.dev("x", -1))]
    join(2, 1)
    final.append(net.push(sib.at[2, t], f_prev.at[t], net.dev("x", 1)))
    yield
    top.wait_recv()
    sib[1, :half] = sib[1, :half] + q_top[...].astype(F32)
    final.append(net.push(sib.at[1, t], f_next.at[t], net.dev("x", -1)))
    low.wait_recv()
    sib[2, half:] = sib[2, half:] + q_low[...].astype(F32)
    final.append(net.push(sib.at[2, b], f_prev.at[b], net.dev("x", 1)))
    yield
    join(3, 0)
    yield
    for copy in final:
        copy.wait_recv()
    sib[3] = sib[3] + f_next[...] + f_prev[...]
    out(sib.at[3])


PLANE_SCRATCH = [((5, 112, WIDTH), BF16), ((5, 112, WIDTH), BF16), ((5, 224, WIDTH), BF16), ((5, 224, WIDTH), BF16)]


def row_scratch(n):
    return [((4, 512, n), F32), ((512, n), BF16), ((256, n), BF16), ((256, n), BF16), ((512, n), F32),
            ((512, n), F32)]


def doc_start(spot, docs):
    start, end = jnp.zeros_like(spot), 0
    for d in range(4):
        end = end + docs[d]
        start = jnp.where(spot >= end, end, start)
    return start


def fold(a):
    return a[:, :128] + a[:, 128:]


def whole_kernel(docs, tok, row_gain, grad, wq, wk, wv, wo,
                 layer_out, token_grad, gain_grad, wq_grad, wk_grad, wv_grad, wo_grad,
                 tok3, grad3, wqkv, wo3, norm_t, kv, qs, gs, big, mix, own_grad, part_a, part_b, inv, qkv, dkv,
                 att, att_t, dq, keep, give, got, own_stats, stats, gain, inner, gains, inners, gain_all, gain_rows,
                 *rest):
    planes = [rest[4 * i:4 * i + 4] for i in range(4)]
    rows = [rest[16 + 6 * i:22 + 6 * i] for i in range(3)]
    send, recv, here, away = rest[34:]
    net = Net(send, recv)
    r, c = net.r, net.c
    slot = pl.multiple_of(c // 2 * HEAD_DIM, HEAD_DIM)
    wk_own, wv_own = wk.at[:, pl.ds(slot, HEAD_DIM)], wv.at[:, pl.ds(slot, HEAD_DIM)]
    q_at, k_at, v_at = (wqkv.at[r, :, pl.ds(0, 256)], wqkv.at[r, :, pl.ds(256, 128)],
                        wqkv.at[r, :, pl.ds(384, 128)])
    others = [(r, lax.rem(c + d, 16)) for d in range(1, 16)]
    peers = [(lax.rem(r + d, 8), c) for d in range(1, 8)]
    live = []

    def step(some=None):
        for s in list(live):
            if some is None or s in some:
                try:
                    next(s)
                except StopIteration:
                    live.remove(s)

    def start(*streams):
        for s in streams:
            next(s)
            live.append(s)

    def at3(ref):
        return lambda i, lo, n: ref.at[i, pl.ds(lo, n)]

    def whole(ref, m):
        return lambda i, lo, n: ref.at[i, pl.ds(lo, m if n is None else n)]

    ins = []
    for i, (src, dst) in enumerate([
            (tok, tok3.at[c, pl.ds(0, BLOCK)]), (grad, grad3.at[c]), (wq, q_at), (wk_own, k_at), (wv_own, v_at),
            (wo, wo3.at[r])]):
        ins.append(pltpu.make_async_copy(src, dst, here.at[i]))
        ins[-1].start()
    tok3[c, BLOCK:BLOCK + EXTRA, :] = jnp.broadcast_to(row_gain[...], (EXTRA, WIDTH))
    net.greet(others + peers)
    ins[0].wait()
    t_lane, g_lane, w_lane, o_lane, k_lane = (Lane(net) for _ in range(5))
    tokens = (gather_plane(t_lane, at3(tok3), 0, 224, 112, "y"), gather_plane(t_lane, at3(tok3), 224, 240, 112, "z"))
    w_share = gather_row(w_lane, [(wq, q_at), (wk_own, k_at), (wv_own, v_at)], whole(wqkv, 512), 256)
    grads = (gather_plane(g_lane, at3(grad3), 0, 224, 112, "y"), gather_plane(g_lane, at3(grad3), 224, 224, 112, "z"))
    o_share = gather_row(o_lane, [(wo, wo3.at[r])], whole(wo3, 256), 128)
    start(*tokens, w_share)
    for copy in ins[1:]:
        copy.wait()
    for some in (tokens, tokens, (w_share,), tokens, tokens, (w_share,)):
        step(some)
    start(*grads, o_share)
    for some in (tokens, grads, (w_share,), grads, (o_share,), tokens, (w_share,), grads, (o_share,)):
        step(some)

    part_a[...] = jnp.zeros_like(part_a)

    @pl.loop(0, 16)
    def _(i):
        t = tok3[i, :BLOCK, :].astype(F32)
        part_a[...] += fold(t * t)

    scale = lax.rsqrt(jnp.sum(part_a[...], axis=1, keepdims=True) * (1.0 / 4096) + eps)
    inv[...] = jnp.broadcast_to(scale, inv.shape)
    qkv[...] = jnp.zeros_like(qkv)

    for piece in range(2):

        @pl.loop(4 * piece, 4 * piece + 4)
        def _(i):
            both = []
            for j in range(2):
                t = tok3[2 * i + j, :BLOCK, :].astype(F32) * jnp.concatenate([inv[...], inv[...]], axis=1)
                n = (t * tok3[2 * i + j, BLOCK:BLOCK + 1, :].astype(F32)).astype(BF16)
                norm_t[2 * i + j] = n.T
                both.append(n)
            qkv[...] += jnp.dot(jnp.concatenate(both, axis=1), wqkv[i], preferred_element_type=F32)

        if piece == 0:
            step(grads)

    kv[r] = qkv[:, 256:].astype(BF16)
    qs[r] = qkv[:, :256].astype(BF16)
    kv_share = gather_row(k_lane, [(kv.at[r], kv.at[r])], whole(kv, BLOCK), 224)
    q_share = gather_row(net, [(qs.at[r], qs.at[r])], whole(qs, BLOCK), 224)
    start(kv_share)
    step(grads)
    step((kv_share,))
    while any(g in live for g in grads + (o_share,)):
        step(grads + (o_share,))

    part = qkv.at[:, pl.ds(0, 256)]
    part[...] = jnp.zeros((BLOCK, 256), F32)

    @pl.loop(0, 8)
    def _(i):
        part[...] += (lax.dot_general(grad3[2 * i], wo3[i, :, :256], NT, preferred_element_type=F32)
                      + lax.dot_general(grad3[2 * i + 1], wo3[i, :, 256:], NT, preferred_element_type=F32))

    gs[r] = qkv[:, :256].astype(BF16)
    gathered = net.total
    g_share = gather_row(net, [(gs.at[r], gs.at[r])], whole(gs, BLOCK), 224)
    start(g_share, q_share)
    while kv_share in live:
        step((kv_share,))

    base = r * BLOCK
    low = jnp.maximum(r - 4, 0) * BLOCK // TILE
    count = (base + BLOCK + TILE - 1) // TILE - low
    spot = base + lax.broadcasted_iota(jnp.int32, (BLOCK, 1), 0)
    first = doc_start(spot, docs)
    lane = lax.broadcasted_iota(jnp.int32, (BLOCK, 128), 1)
    table = jnp.zeros((BLOCK, 128), F32)

    def keys(i):
        return pl.ds(pl.multiple_of((low + i) * TILE, TILE), TILE)

    def slot_of(h, i):
        return pl.ds(pl.multiple_of((10 * h + i) * BLOCK, 64), BLOCK)

    def lot(base, i, m=512):
        return pl.ds(pl.multiple_of(base + i * m, 256), m)

    flat = kv.reshape(8 * BLOCK, 256)
    heads = tuple(enumerate((part_a, part_b)))
    q = [qs[r, :, h * 128:(h + 1) * 128] for h in range(2)]
    part_a[...] = jnp.full_like(part_a, -1e30)
    part_b[...] = jnp.full_like(part_b, -1e30)

    @pl.loop(0, count)
    def _(i):
        key = (low + i) * TILE + lax.broadcasted_iota(jnp.int32, (1, TILE), 1)
        seen = (key <= spot) & (key >= first)
        for h, part in heads:
            s = lax.dot_general(q[h], flat[keys(i), :128], NT, preferred_element_type=F32) * FACTOR
            s = jnp.where(seen, s, -1e30)
            big[slot_of(h, i), :] = s
            part[...] = jnp.maximum(part[...], jnp.maximum(s[:, :128], s[:, 128:]))

    m = [jnp.max(part[...], axis=1, keepdims=True) for _, part in heads]
    part_a[...] = jnp.zeros_like(part_a)
    part_b[...] = jnp.zeros_like(part_b)

    @pl.loop(0, count)
    def _(i):
        for h, part in heads:
            e = jnp.exp(big[slot_of(h, i), :] - m[h])
            big[slot_of(h, i), :] = e
            part[...] += fold(e)

    over = [1.0 / jnp.sum(part[...], axis=1, keepdims=True) for _, part in heads]
    step((g_share,))
    g = [gs[r, :, h * 128:(h + 1) * 128] for h in range(2)]
    slope = (keep, give)
    for ref in (part_a, part_b, keep, give):
        ref[...] = jnp.zeros_like(ref)

    @pl.loop(0, count)
    def _(i):
        for h, part in heads:
            dp = lax.dot_general(g[h], flat[keys(i), 128:], NT, preferred_element_type=F32)
            p = big[slot_of(h, i), :] * over[h]
            slope[h][...] += fold(p * dp)
            part[...] += jnp.dot(p.astype(BF16), flat[keys(i), 128:], preferred_element_type=F32)

    w = [jnp.sum(ref[...], axis=1, keepdims=True) for ref in slope]
    for h, part in heads:
        att[:, h * 128:(h + 1) * 128] = part[...].astype(BF16)
        att_t[h * 128:(h + 1) * 128, :] = part[...].T.astype(BF16)
    step((g_share,))

    def put_layer(lo, n, total):
        layer_out[lo:lo + n] = (tok3[c, lo:lo + n, :].astype(F32) + total).astype(BF16)

    def put_grad(lo, n, total):
        token_grad[lo:lo + n] = total

    outs = []

    def put_out(src, dst):
        outs.append(pltpu.make_async_copy(src, dst, away.at[len(outs)]))
        outs[-1].start()

    def put_wo(total):
        put_out(total.at[pl.ds(0, 256)], wo_grad.at[:, pl.ds(0, 256)])
        put_out(total.at[pl.ds(256, 256)], wo_grad.at[:, pl.ds(256, 256)])

    def put_wq(total):
        put_out(total, wq_grad)

    def put_kv(total):
        side = total[...].T
        wk_grad[...] = side[:64]
        wv_grad[...] = side[64:]

    @pl.loop(0, 8)
    def _(i):
        mix[2 * i] = jnp.dot(att[...], wo3[i, :, :256], preferred_element_type=F32).astype(BF16)
        mix[2 * i + 1] = jnp.dot(att[...], wo3[i, :, 256:], preferred_element_type=F32).astype(BF16)

    m_lane = Lane(net, t_lane)
    mixes = (scatter_plane(m_lane, mix, *planes[0], 0, 112, "y", put_layer),
             scatter_plane(m_lane, mix, *planes[1], 224, 112, "z", put_layer))
    start(*mixes)

    @pl.loop(0, 16)
    def _(i):
        big[lot(20 * BLOCK, i, 256), :] = jnp.dot(att_t[...], grad3[i], preferred_element_type=F32)

    s_lane = Lane(net, w_lane)
    wo_sum = scatter_row(s_lane, lambda x, k: big.at[lot(20 * BLOCK, 2 * x + k)], *rows[0], put_wo)
    start(wo_sum)

    step((g_share, q_share))

    part_a[...] = jnp.zeros_like(part_a)
    part_b[...] = jnp.zeros_like(part_b)

    def slopes(some):
        @pl.loop(*some)
        def _(i):
            for h, part in heads:
                dp = lax.dot_general(g[h], flat[keys(i), 128:], NT, preferred_element_type=F32)
                d = (big[slot_of(h, i), :] * over[h] * (dp - w[h]) * FACTOR).astype(BF16)
                part[...] += jnp.dot(d, flat[keys(i), :128], preferred_element_type=F32)

    slopes((0, count // 2))
    step((wo_sum,))
    step(mixes)
    step((g_share, q_share))
    slopes((count // 2, count))
    step((g_share, q_share))
    for h, part in heads:
        dq[:, h * 128:(h + 1) * 128] = part[...].astype(BF16)
        for j, v in enumerate((m[h], over[h], w[h])):
            table = jnp.where(lane == 3 * h + j, v, table)
    own_stats[...] = table.T[:8, :]
    told = [net.push(own_stats, stats.at[r], p) for p in peers]
    stats[r] = own_stats[...]

    @pl.loop(0, 16)
    def _(i):
        big[lot(0, i, 256), :] = jnp.dot(norm_t[i], dq[...], preferred_element_type=F32)

    wq_sum = scatter_row(s_lane, lambda x, k: big.at[lot(0, 2 * x + k)], *rows[1], put_wq)
    start(wq_sum)
    step((wo_sum,))
    while q_share in live or g_share in live:
        step((q_share, g_share))
    for copy in told:
        copy.wait_recv()

    key = base + lax.broadcasted_iota(jnp.int32, (BLOCK, 1), 0)
    k, v = kv[r, :, :128], kv[r, :, 128:]
    sums = [(ref, at) for at in (0, 128) for ref in (qkv.at[:, pl.ds(at, 128)], qkv.at[:, pl.ds(256 + at, 128)])]
    qkv[...] = jnp.zeros_like(qkv)
    for b in range(5):

        @pl.when(r + b < 8)
        def _():
            o = r + b
            row = o * BLOCK + lax.broadcasted_iota(jnp.int32, (1, BLOCK), 1)
            seen = (key <= row) & (key >= doc_start(row, docs))
            for h in range(2):
                cols = slice(h * 128, (h + 1) * 128)
                more = slice(256 + h * 128, 256 + (h + 1) * 128)
                q, g = qs[o, :, cols], gs[o, :, cols]
                m, over, w = (stats[o, 3 * h + j:3 * h + j + 1, :] for j in range(3))
                s = lax.dot_general(k, q, NT, preferred_element_type=F32) * FACTOR
                p = jnp.exp(jnp.where(seen, s, -1e30) - m) * over
                dp = lax.dot_general(v, g, NT, preferred_element_type=F32)
                d = (p * (dp - w) * FACTOR).astype(BF16)
                qkv[:, more] += jnp.dot(p.astype(BF16), g, preferred_element_type=F32)
                qkv[:, cols] += jnp.dot(d, q, preferred_element_type=F32)

        if b == 0:
            step(mixes)
        if b == 2:
            step((wq_sum,))
            step(mixes)

    two = [qkv[:, at:at + 128].astype(BF16).astype(F32) + qkv[:, at + 128:at + 256].astype(BF16).astype(F32)
           for at in (0, 256)]
    for j, value in enumerate(two):
        upper = value.astype(BF16)
        dkv[:, j * 128:(j + 1) * 128] = upper
        dkv[:, 256 + j * 128:256 + (j + 1) * 128] = (value - upper.astype(F32)).astype(BF16)
    even = lax.rem(c, 2) == 0
    left = jnp.concatenate([two[0][:, :64], two[1][:, :64]], axis=1)
    right = jnp.concatenate([two[0][:, 64:], two[1][:, 64:]], axis=1)
    keep[...] = jnp.where(even, left, right)
    give[...] = jnp.where(even, right, left)
    swap = net.push(give, got, (r, c + 1 - 2 * lax.rem(c, 2)))

    own_grad[...] = grad3[c]
    net.finish(gathered)
    ngrad = grad3
    part_a[...] = jnp.zeros_like(part_a)
    for piece in range(2):

        @pl.loop(4 * piece, 4 * piece + 4)
        def _(i):
            for j in range(2):
                at = pl.ds(j * 256, 256)
                g = lax.dot_general(dq[...], wqkv[i, at, :256], NT, preferred_element_type=F32)
                for h in range(2):
                    g += lax.dot_general(dkv[:, h * 256:(h + 1) * 256], wqkv[i, at, 256:], NT,
                                         preferred_element_type=F32)
                ngrad[2 * i + j] = g.astype(BF16)
                a = g * tok3[2 * i + j, :BLOCK, :].astype(F32)
                part_a[...] += fold(a * tok3[2 * i + j, BLOCK:BLOCK + 1, :].astype(F32))
                a = a * jnp.concatenate([inv[...], inv[...]], axis=1)
                gain[2 * i + j] = jnp.broadcast_to(jnp.sum(a, axis=0, keepdims=True), (8, WIDTH))

        step((wq_sum,) if piece == 0 else (wo_sum,))

    inner[...] = jnp.broadcast_to(jnp.sum(part_a[...].T, axis=0, keepdims=True), inner.shape)
    small = []
    for d, dev in enumerate(others):
        small.append(net.push(gain.at[lax.rem(c + d + 1, 16), pl.ds(0, 1)], gains.at[d, pl.ds(0, 1)], dev))
        small.append(net.push(inner.at[pl.ds(0, 1)], inners.at[d, pl.ds(0, 1)], dev))
    earlier = net.total
    n_lane = Lane(net, g_lane)
    ngs = (scatter_plane(n_lane, ngrad, *planes[2], 0, 112, "y", put_grad),
           scatter_plane(n_lane, ngrad, *planes[3], 224, 112, "z", put_grad))
    start(*ngs)
    swap.wait_recv()
    four = keep[...] + got[...]
    upper = four.astype(BF16)
    dkv[:, :128] = upper
    dkv[:, 128:256] = (four - upper.astype(F32)).astype(BF16)

    @pl.loop(0, 4)
    def _(i):
        for j in range(4):
            t = jnp.dot(norm_t[4 * i + j], dkv[:, :256], preferred_element_type=F32)
            rows_at = pl.ds(pl.multiple_of(4096 + (j % 2) * 256 + i * 512, 256), 256)
            big[rows_at, (j // 2) * 128:(j // 2) * 128 + 128] = fold(t)

    e_lane = Lane(net, o_lane, k_lane)
    kv_sum = scatter_row(e_lane, lambda x, k: big.at[lot(4096, x), pl.ds(pl.multiple_of(k * 128, 128), 128)],
                         *rows[2], put_kv)
    start(kv_sum)
    for some in (mixes, ngs, (kv_sum,)):
        step(some)
    for copy in small:
        copy.wait_recv()
    g, total = gain[c, 0:1, :], inner[0:1, :]
    for d in range(15):
        g = g + gains[d, 0:1, :]
        total = total + inners[d, 0:1, :]
    gain_all[...] = jnp.broadcast_to(g, gain_all.shape)
    final = [e_lane.push(gain_all.at[pl.ds(0, 1)], gain_rows.at[d, pl.ds(0, 1)], dev) for d, dev in enumerate(peers)]
    net.finish(earlier)
    for some in ((wo_sum,), (wq_sum,), (kv_sum,), ngs, (kv_sum,), (wq_sum,), ngs):
        step(some)
    while live:
        step()
    for copy in final:
        copy.wait_recv()
    for d in range(7):
        g = g + gain_rows[d, 0:1, :]
    gain_grad[...] = g
    mean = jnp.broadcast_to(total, (128, BLOCK)).T * (1.0 / 4096)
    mean = jnp.concatenate([mean, mean], axis=1)
    i = jnp.concatenate([inv[...], inv[...]], axis=1)
    scaled = token_grad[...] * tok3[c, BLOCK:BLOCK + 1, :].astype(F32)
    token_grad[...] = own_grad[...].astype(F32) + i * scaled - tok3[c, :BLOCK, :].astype(F32) * i**3 * mean
    for copy in outs:
        copy.wait()
    net.finish()


def whole_layer(*operands):
    copies = 4 * 30 + 21 + 4 * 11 + 7 + 1 + 30
    scratch = [
        ((16, BLOCK + EXTRA, WIDTH), BF16), ((16, BLOCK, WIDTH), BF16), ((8, 512, 512), BF16), ((8, 256, 512), BF16),
        ((16, WIDTH, BLOCK), BF16), ((8, BLOCK, 256), BF16), ((8, BLOCK, 256), BF16), ((8, BLOCK, 256), BF16),
        ((20 * BLOCK + 4096, 256), F32), ((16, BLOCK, WIDTH), BF16), ((BLOCK, WIDTH), BF16),
        ((BLOCK, 128), F32), ((BLOCK, 128), F32), ((BLOCK, 128), F32), ((BLOCK, 512), F32), ((BLOCK, 512), BF16),
        ((BLOCK, 256), BF16), ((256, BLOCK), BF16), ((BLOCK, 256), BF16), ((BLOCK, 128), F32), ((BLOCK, 128), F32),
        ((BLOCK, 128), F32), ((8, BLOCK), F32), ((8, 8, BLOCK), F32), ((16, 8, WIDTH), F32), ((8, BLOCK), F32),
        ((15, 8, WIDTH), F32), ((15, 8, BLOCK), F32), ((8, WIDTH), F32), ((7, 8, WIDTH), F32),
    ] + PLANE_SCRATCH * 4 + row_scratch(256) * 2 + row_scratch(128)
    return pl.pallas_call(
        whole_kernel,
        out_shape=[
            jax.ShapeDtypeStruct((BLOCK, WIDTH), BF16), jax.ShapeDtypeStruct((BLOCK, WIDTH), F32),
            jax.ShapeDtypeStruct((1, WIDTH), F32), jax.ShapeDtypeStruct((512, 256), F32),
            jax.ShapeDtypeStruct((64, 512), F32), jax.ShapeDtypeStruct((64, 512), F32),
            jax.ShapeDtypeStruct((256, 512), F32),
        ],
        in_specs=[SMEM, ANY, VM] + [ANY] * 5,
        out_specs=[VM, VM, VM, ANY, VM, VM, ANY],
        scratch_shapes=[pltpu.VMEM(*b) for b in scratch] + [
            pltpu.SemaphoreType.DMA((POOL,)), pltpu.SemaphoreType.DMA((copies,)), pltpu.SemaphoreType.DMA((6,)),
            pltpu.SemaphoreType.DMA((3,))],
        compiler_params=pltpu.CompilerParams(collective_id=1, has_side_effects=True, vmem_limit_bytes=VMEM_MOST),
        name="whole_layer",
    )(*operands)


def hand_kernel(*refs):
    for src, dst in zip(refs[:7], refs[7:]):
        dst[...] = src[...]


def hand_over(*arrays):
    return pl.pallas_call(
        hand_kernel,
        out_shape=[jax.ShapeDtypeStruct(a.shape, a.dtype) for a in arrays],
        in_specs=[VM] * 7,
        out_specs=[VM] * 7,
        name="hand_over",
    )(*arrays)


def body(tokens, norm_gain, w_query, w_key, w_value, w_out, out_grad, doc_lengths):
    layer_out, token_grad, gain_grad, wq_grad, wk_grad, wv_grad, wo_grad = hand_over(*whole_layer(
        doc_lengths, tokens, norm_gain.reshape(1, WIDTH), out_grad, w_query, w_key, w_value, w_out))
    return layer_out, token_grad, gain_grad.reshape(WIDTH), wq_grad, wk_grad.T, wv_grad.T, wo_grad


def solution(mesh):
    in_specs = (P("row", "col"), P("col"), P("row", "col"), P("row", None), P("row", None),
                P("col", "row"), P("row", "col"), P())
    out_specs = (P("row", "col"), P("row", "col"), P("col"), P("row", "col"), P("row", "col"),
                 P("row", "col"), P("col", "row"))
    return jax.shard_map(body, mesh=mesh, in_specs=in_specs, out_specs=out_specs, check_vma=False)
```

```python
import functools

import jax
import jax.numpy as jnp
from jax import lax
from jax.experimental import pallas as pl
from jax.experimental.pallas import tpu as pltpu
from jax.sharding import PartitionSpec as P

HEAD_DIM = 128
BLOCK = 448
EXTRA = 16
WIDTH = 256
TILE = 256
MOST_TILES = 10
eps = 1e-05
FACTOR = HEAD_DIM ** (-0.5)
F32 = jnp.float32
BF16 = jnp.bfloat16
ANY = pl.BlockSpec(memory_space=pl.ANY)
SMEM = pl.BlockSpec(memory_space=pltpu.SMEM)
VM = pl.BlockSpec(memory_space=pltpu.VMEM)
VMEM_MOST = 67043328
NT = (((1,), (1,)), ((), ()))


POOL = 100


class Net:
    def __init__(self, send, recv):
        self.send, self.recv, self.used, self.open, self.total = send, recv, 0, [], 0
        self.r, self.c = lax.axis_index("row"), lax.axis_index("col")
        self.x, self.k = self.r // 2, lax.rem(self.r, 2)
        self.y, self.z = self.c // 4, lax.rem(self.c, 4)

    def dev(self, axis, step=1):
        if axis == "k":
            return (self.x * 2 + 1 - self.k, self.c)
        if axis == "x":
            return (lax.rem(self.x + step + 4, 4) * 2 + self.k, self.c)
        if axis == "y":
            return (self.r, self.col(step, 0))
        return (self.r, self.col(0, step))

    def col(self, dy, dz):
        return lax.rem(self.y + dy + 4, 4) * 4 + lax.rem(self.z + dz + 4, 4)

    def greet(self, devices):
        bar = pltpu.get_barrier_semaphore()
        for d in devices:
            pl.semaphore_signal(bar, inc=1, device_id=d, device_id_type=pl.DeviceIdType.MESH)
        pl.semaphore_wait(bar, len(devices))

    def push(self, src, dst, device, slot=None):
        if slot is None:
            slot = self.used
            self.used += 1
        if len(self.open) >= POOL:
            self.open.pop(0)[1].wait_send()
        copy = pltpu.make_async_remote_copy(
            src_ref=src, dst_ref=dst, send_sem=self.send.at[self.total % POOL], recv_sem=self.recv.at[slot],
            device_id=device, device_id_type=pl.DeviceIdType.MESH)
        copy.start()
        self.open.append((self.total, copy))
        self.total += 1
        return copy

    def finish(self, count=None):
        while self.open and (count is None or self.open[0][0] < count):
            self.open.pop(0)[1].wait_send()


class Lane:
    def __init__(self, net, *before):
        self.net, self.mine = net, []
        self.old = [slot for lane in before for slot in lane.mine]

    def __getattr__(self, name):
        return getattr(self.net, name)

    def push(self, src, dst, device):
        slot = self.old.pop(0) if self.old else None
        self.mine.append(self.net.used if slot is None else slot)
        return self.net.push(src, dst, device, slot)


def gather_plane(net, at, low, count, half, first):
    second = "z" if first == "y" else "y"
    top, bot = (low, half), (low + half, count - half)
    rest = []

    def blk(da, db, rows):
        dy, dz = (da, db) if first == "y" else (db, da)
        return at(net.col(dy, dz), *rows)

    def push(da, db, rows, axis, way):
        copy = net.push(blk(da, db, rows), blk(da, db, rows), net.dev(axis, way))
        rest.append(copy)
        return copy

    def recv(copy):
        rest[:] = [other for other in rest if other is not copy]
        copy.wait_recv()

    a_next, a_prev = push(0, 0, top, first, 1), push(0, 0, bot, first, -1)
    nexts, prevs = {0: push(0, 0, top, second, 1)}, {0: push(0, 0, bot, second, -1)}
    a_next2, a_prev2 = push(0, 0, bot, first, 1), push(0, 0, top, first, -1)
    push(0, 0, bot, second, 1)
    push(0, 0, top, second, -1)

    def relay(u):
        recv(nexts[u])
        push(u, -1, top, second, 1)
        recv(prevs[u])
        push(u, 1, bot, second, -1)

    yield
    recv(a_next)
    f_next = push(-1, 0, top, first, 1)
    nexts[-1] = push(-1, 0, top, second, 1)
    recv(a_prev)
    f_prev = push(1, 0, bot, first, -1)
    prevs[1] = push(1, 0, bot, second, -1)
    relay(0)
    yield
    recv(a_next2)
    prevs[-1] = push(-1, 0, bot, second, -1)
    push(-1, 0, bot, second, 1)
    push(-1, 0, top, second, -1)
    recv(a_prev2)
    nexts[1] = push(1, 0, top, second, 1)
    push(1, 0, bot, second, 1)
    push(1, 0, top, second, -1)
    yield
    recv(f_next)
    nexts[2] = push(2, 0, top, second, 1)
    recv(f_prev)
    prevs[2] = push(2, 0, bot, second, -1)
    push(2, 0, bot, second, 1)
    push(2, 0, top, second, -1)
    yield
    relay(-1)
    relay(1)
    yield
    relay(2)
    yield
    for copy in rest:
        copy.wait_recv()


def gather_row(net, parts, at, half):
    def send(way, lo):
        return [net.push(s.at[pl.ds(lo, half)], d.at[pl.ds(lo, half)], net.dev("x", way)) for s, d in parts]

    def blk(dx, lo=0, n=None):
        return at(lax.rem(net.x + dx + 4, 4) * 2 + net.k, lo, n)

    def push(dx, device, lo=0, n=None):
        return net.push(blk(dx, lo, n), blk(dx, lo, n), device)

    def recv(copies):
        for c in copies:
            c.wait_recv()

    sent = [send(1, 0), send(-1, half), send(1, half), send(-1, 0)]
    tail = [net.push(s, d, net.dev("k")) for s, d in parts]
    yield
    recv(sent[0])
    f_next = push(-1, net.dev("x", 1), 0, half)
    recv(sent[1])
    f_prev = push(1, net.dev("x", -1), half, half)
    yield
    recv(sent[2])
    tail.append(push(-1, net.dev("k")))
    recv(sent[3])
    tail.append(push(1, net.dev("k")))
    yield
    f_next.wait_recv()
    tail.append(push(2, net.dev("k"), 0, half))
    f_prev.wait_recv()
    tail.append(push(2, net.dev("k"), half, half))
    yield
    recv(tail)


def scatter_plane(net, src, q_top, q_low, f_next, f_prev, low, half, first, out):
    second = "z" if first == "y" else "y"
    units = (2, -1, 1, 0)
    t, b = pl.ds(0, half), pl.ds(half, half)

    def col(da, db):
        dy, dz = (db, da) if first == "y" else (da, db)
        return net.col(dy, dz)

    def at(da, db, lo):
        return src.at[col(da, db), pl.ds(low + lo, half)]

    def add(da, db, lo, value):
        rows = slice(low + lo, low + lo + half)
        i = col(da, db)
        src[i, rows, :] = (src[i, rows, :].astype(F32) + value.astype(F32)).astype(BF16)

    tops, lows, waits = {}, {}, {}
    for i, u in enumerate(units):
        tops[u] = net.push(at(u, 2, 0), q_top.at[i], net.dev(first, -1))
        lows[u] = net.push(at(u, 2, half), q_low.at[i], net.dev(first, 1))
    for i, u in enumerate(units):
        waits[u] = [net.push(at(u, -1, half), f_next.at[i, b], net.dev(first, -1)),
                    net.push(at(u, 1, 0), f_prev.at[i, t], net.dev(first, 1))]
    yield
    for i, u in enumerate(units):
        tops[u].wait_recv()
        add(u, -1, 0, q_top[i])
        waits[u].append(net.push(at(u, -1, 0), f_next.at[i, t], net.dev(first, -1)))
        lows[u].wait_recv()
        add(u, 1, half, q_low[i])
        waits[u].append(net.push(at(u, 1, half), f_prev.at[i, b], net.dev(first, 1)))
    yield

    def total(i, u):
        for copy in waits[u]:
            copy.wait_recv()
        rows = slice(low, low + 2 * half)
        return src[col(u, 0), rows, :].astype(F32) + f_next[i].astype(F32) + f_prev[i].astype(F32)

    def settle(i, u):
        value = total(i, u).astype(BF16)
        src[col(u, 0), low:low + 2 * half, :] = value

    settle(0, 2)
    top = net.push(at(2, 0, 0), q_top.at[4], net.dev(second, -1))
    bot = net.push(at(2, 0, half), q_low.at[4], net.dev(second, 1))
    settle(1, -1)
    final = [net.push(at(-1, 0, half), f_next.at[4, b], net.dev(second, -1))]
    settle(2, 1)
    final.append(net.push(at(1, 0, 0), f_prev.at[4, t], net.dev(second, 1)))
    yield
    top.wait_recv()
    add(-1, 0, 0, q_top[4])
    final.append(net.push(at(-1, 0, 0), f_next.at[4, t], net.dev(second, -1)))
    bot.wait_recv()
    add(1, 0, half, q_low[4])
    final.append(net.push(at(1, 0, half), f_prev.at[4, b], net.dev(second, 1)))
    yield
    last = total(3, 0)
    for copy in final:
        copy.wait_recv()
    out(low, 2 * half, last + f_next[4].astype(F32) + f_prev[4].astype(F32))


def scatter_row(net, at, sib, far, q_top, q_low, f_next, f_prev, out):
    half = 256
    t, b = pl.ds(0, half), pl.ds(half, half)

    def block(dx, k):
        return at(lax.rem(net.x + dx + 4, 4), k)

    pair = [net.push(block(u, 1 - net.k), sib.at[i], net.dev("k")) for i, u in enumerate((2, -1, 1, 0))]

    def join(i, u):
        pair[i].wait_recv()
        sib[i] = sib[i] + block(u, net.k)[...]

    yield
    join(0, 2)
    far[...] = sib[0].astype(BF16)
    top = net.push(far.at[t], q_top, net.dev("x", -1))
    low = net.push(far.at[b], q_low, net.dev("x", 1))
    join(1, -1)
    final = [net.push(sib.at[1, b], f_next.at[b], net.dev("x", -1))]
    join(2, 1)
    final.append(net.push(sib.at[2, t], f_prev.at[t], net.dev("x", 1)))
    yield
    top.wait_recv()
    sib[1, :half] = sib[1, :half] + q_top[...].astype(F32)
    final.append(net.push(sib.at[1, t], f_next.at[t], net.dev("x", -1)))
    low.wait_recv()
    sib[2, half:] = sib[2, half:] + q_low[...].astype(F32)
    final.append(net.push(sib.at[2, b], f_prev.at[b], net.dev("x", 1)))
    yield
    join(3, 0)
    yield
    for copy in final:
        copy.wait_recv()
    sib[3] = sib[3] + f_next[...] + f_prev[...]
    out(sib.at[3])


PLANE_SCRATCH = [((5, 112, WIDTH), BF16), ((5, 112, WIDTH), BF16), ((5, 224, WIDTH), BF16), ((5, 224, WIDTH), BF16)]


def row_scratch(n):
    return [((4, 512, n), F32), ((512, n), BF16), ((256, n), BF16), ((256, n), BF16), ((512, n), F32),
            ((512, n), F32)]


def doc_start(spot, docs):
    start, end = jnp.zeros_like(spot), 0
    for d in range(4):
        end = end + docs[d]
        start = jnp.where(spot >= end, end, start)
    return start


def fold(a):
    return a[:, :128] + a[:, 128:]


def whole_kernel(docs, tok, row_gain, grad, wq, wk, wv, wo,
                 layer_out, token_grad, gain_grad, wq_grad, wk_grad, wv_grad, wo_grad,
                 tok3, grad3, wqkv, wo3, norm_t, kv, qs, gs, big, mix, own_grad, part_a, part_b, inv, qkv, dkv,
                 att, att_t, dq, keep, give, got, own_stats, stats, gain, inner, gains, inners, gain_all, gain_rows,
                 *rest):
    planes = [rest[4 * i:4 * i + 4] for i in range(4)]
    rows = [rest[16 + 6 * i:22 + 6 * i] for i in range(3)]
    send, recv, here, away = rest[34:]
    net = Net(send, recv)
    r, c = net.r, net.c
    slot = pl.multiple_of(c // 2 * HEAD_DIM, HEAD_DIM)
    wk_own, wv_own = wk.at[:, pl.ds(slot, HEAD_DIM)], wv.at[:, pl.ds(slot, HEAD_DIM)]
    q_at, k_at, v_at = (wqkv.at[r, :, pl.ds(0, 256)], wqkv.at[r, :, pl.ds(256, 128)],
                        wqkv.at[r, :, pl.ds(384, 128)])
    others = [(r, lax.rem(c + d, 16)) for d in range(1, 16)]
    peers = [(lax.rem(r + d, 8), c) for d in range(1, 8)]
    live = []

    def step(some=None):
        for s in list(live):
            if some is None or s in some:
                try:
                    next(s)
                except StopIteration:
                    live.remove(s)

    def start(*streams):
        for s in streams:
            next(s)
            live.append(s)

    def at3(ref):
        return lambda i, lo, n: ref.at[i, pl.ds(lo, n)]

    def whole(ref, m):
        return lambda i, lo, n: ref.at[i, pl.ds(lo, m if n is None else n)]

    ins = []
    for i, (src, dst) in enumerate([
            (tok, tok3.at[c, pl.ds(0, BLOCK)]), (grad, grad3.at[c]), (wq, q_at), (wk_own, k_at), (wv_own, v_at),
            (wo, wo3.at[r])]):
        ins.append(pltpu.make_async_copy(src, dst, here.at[i]))
        ins[-1].start()
    tok3[c, BLOCK:BLOCK + EXTRA, :] = jnp.broadcast_to(row_gain[...].reshape(1, WIDTH), (EXTRA, WIDTH))
    net.greet(others + peers)
    ins[0].wait()
    t_lane, g_lane, w_lane, o_lane, k_lane = (Lane(net) for _ in range(5))
    tokens = (gather_plane(t_lane, at3(tok3), 0, 224, 112, "y"), gather_plane(t_lane, at3(tok3), 224, 240, 112, "z"))
    w_share = gather_row(w_lane, [(wq, q_at), (wk_own, k_at), (wv_own, v_at)], whole(wqkv, 512), 256)
    grads = (gather_plane(g_lane, at3(grad3), 0, 224, 112, "y"), gather_plane(g_lane, at3(grad3), 224, 224, 112, "z"))
    o_share = gather_row(o_lane, [(wo, wo3.at[r])], whole(wo3, 256), 128)
    start(*tokens, w_share)
    for copy in ins[1:]:
        copy.wait()
    for some in (tokens, tokens, (w_share,), tokens, tokens, (w_share,)):
        step(some)
    start(*grads, o_share)
    for some in (tokens, grads, (w_share,), grads, (o_share,), tokens, (w_share,), grads, (o_share,)):
        step(some)

    part_a[...] = jnp.zeros_like(part_a)

    @pl.loop(0, 16)
    def _(i):
        t = tok3[i, :BLOCK, :].astype(F32)
        part_a[...] += fold(t * t)

    scale = lax.rsqrt(jnp.sum(part_a[...], axis=1, keepdims=True) * (1.0 / 4096) + eps)
    inv[...] = jnp.broadcast_to(scale, inv.shape)
    qkv[...] = jnp.zeros_like(qkv)

    for piece in range(2):

        @pl.loop(4 * piece, 4 * piece + 4)
        def _(i):
            both = []
            for j in range(2):
                t = tok3[2 * i + j, :BLOCK, :].astype(F32) * jnp.concatenate([inv[...], inv[...]], axis=1)
                n = (t * tok3[2 * i + j, BLOCK:BLOCK + 1, :].astype(F32)).astype(BF16)
                norm_t[2 * i + j] = n.T
                both.append(n)
            qkv[...] += jnp.dot(jnp.concatenate(both, axis=1), wqkv[i], preferred_element_type=F32)

        if piece == 0:
            step(grads)

    kv[r] = qkv[:, 256:].astype(BF16)
    qs[r] = qkv[:, :256].astype(BF16)
    kv_share = gather_row(k_lane, [(kv.at[r], kv.at[r])], whole(kv, BLOCK), 224)
    q_share = gather_row(net, [(qs.at[r], qs.at[r])], whole(qs, BLOCK), 224)
    start(kv_share)
    step(grads)
    step((kv_share,))
    while any(g in live for g in grads + (o_share,)):
        step(grads + (o_share,))

    part = qkv.at[:, pl.ds(0, 256)]
    part[...] = jnp.zeros((BLOCK, 256), F32)

    @pl.loop(0, 8)
    def _(i):
        part[...] += (lax.dot_general(grad3[2 * i], wo3[i, :, :256], NT, preferred_element_type=F32)
                      + lax.dot_general(grad3[2 * i + 1], wo3[i, :, 256:], NT, preferred_element_type=F32))

    gs[r] = qkv[:, :256].astype(BF16)
    gathered = net.total
    g_share = gather_row(net, [(gs.at[r], gs.at[r])], whole(gs, BLOCK), 224)
    start(g_share, q_share)
    while kv_share in live:
        step((kv_share,))

    base = r * BLOCK
    low = jnp.maximum(r - 4, 0) * BLOCK // TILE
    count = (base + BLOCK + TILE - 1) // TILE - low
    spot = base + lax.broadcasted_iota(jnp.int32, (BLOCK, 1), 0)
    first = doc_start(spot, docs)
    lane = lax.broadcasted_iota(jnp.int32, (BLOCK, 128), 1)
    table = jnp.zeros((BLOCK, 128), F32)

    def keys(i):
        return pl.ds(pl.multiple_of((low + i) * TILE, TILE), TILE)

    def slot_of(h, i):
        return pl.ds(pl.multiple_of((10 * h + i) * BLOCK, 64), BLOCK)

    def lot(base, i, m=512):
        return pl.ds(pl.multiple_of(base + i * m, 256), m)

    flat = kv.reshape(8 * BLOCK, 256)
    heads = tuple(enumerate((part_a, part_b)))
    q = [qs[r, :, h * 128:(h + 1) * 128] for h in range(2)]
    part_a[...] = jnp.full_like(part_a, -1e30)
    part_b[...] = jnp.full_like(part_b, -1e30)

    @pl.loop(0, count)
    def _(i):
        key = (low + i) * TILE + lax.broadcasted_iota(jnp.int32, (1, TILE), 1)
        seen = (key <= spot) & (key >= first)
        for h, part in heads:
            s = lax.dot_general(q[h], flat[keys(i), :128], NT, preferred_element_type=F32) * FACTOR
            s = jnp.where(seen, s, -1e30)
            big[slot_of(h, i), :] = s
            part[...] = jnp.maximum(part[...], jnp.maximum(s[:, :128], s[:, 128:]))

    m = [jnp.max(part[...], axis=1, keepdims=True) for _, part in heads]
    part_a[...] = jnp.zeros_like(part_a)
    part_b[...] = jnp.zeros_like(part_b)

    @pl.loop(0, count)
    def _(i):
        for h, part in heads:
            e = jnp.exp(big[slot_of(h, i), :] - m[h])
            big[slot_of(h, i), :] = e
            part[...] += fold(e)

    over = [1.0 / jnp.sum(part[...], axis=1, keepdims=True) for _, part in heads]
    step((g_share,))
    g = [gs[r, :, h * 128:(h + 1) * 128] for h in range(2)]
    slope = (keep, give)
    for ref in (part_a, part_b, keep, give):
        ref[...] = jnp.zeros_like(ref)

    @pl.loop(0, count)
    def _(i):
        for h, part in heads:
            dp = lax.dot_general(g[h], flat[keys(i), 128:], NT, preferred_element_type=F32)
            p = big[slot_of(h, i), :] * over[h]
            slope[h][...] += fold(p * dp)
            part[...] += jnp.dot(p.astype(BF16), flat[keys(i), 128:], preferred_element_type=F32)

    w = [jnp.sum(ref[...], axis=1, keepdims=True) for ref in slope]
    for h, part in heads:
        att[:, h * 128:(h + 1) * 128] = part[...].astype(BF16)
        att_t[h * 128:(h + 1) * 128, :] = part[...].T.astype(BF16)
    step((g_share,))

    def put_layer(lo, n, total):
        layer_out[lo:lo + n] = (tok3[c, lo:lo + n, :].astype(F32) + total).astype(BF16)

    def put_grad(lo, n, total):
        token_grad[lo:lo + n] = total

    outs = []

    def put_out(src, dst):
        outs.append(pltpu.make_async_copy(src, dst, away.at[len(outs)]))
        outs[-1].start()

    def put_wo(total):
        put_out(total.at[pl.ds(0, 256)], wo_grad.at[:, pl.ds(0, 256)])
        put_out(total.at[pl.ds(256, 256)], wo_grad.at[:, pl.ds(256, 256)])

    def put_wq(total):
        put_out(total, wq_grad)

    def put_kv(total):
        side = total[...].T
        wk_grad[...] = side[:64]
        wv_grad[...] = side[64:]

    @pl.loop(0, 8)
    def _(i):
        mix[2 * i] = jnp.dot(att[...], wo3[i, :, :256], preferred_element_type=F32).astype(BF16)
        mix[2 * i + 1] = jnp.dot(att[...], wo3[i, :, 256:], preferred_element_type=F32).astype(BF16)

    m_lane = Lane(net, t_lane)
    mixes = (scatter_plane(m_lane, mix, *planes[0], 0, 112, "y", put_layer),
             scatter_plane(m_lane, mix, *planes[1], 224, 112, "z", put_layer))
    start(*mixes)

    @pl.loop(0, 16)
    def _(i):
        big[lot(20 * BLOCK, i, 256), :] = jnp.dot(att_t[...], grad3[i], preferred_element_type=F32)

    s_lane = Lane(net, w_lane)
    wo_sum = scatter_row(s_lane, lambda x, k: big.at[lot(20 * BLOCK, 2 * x + k)], *rows[0], put_wo)
    start(wo_sum)

    step((g_share, q_share))

    part_a[...] = jnp.zeros_like(part_a)
    part_b[...] = jnp.zeros_like(part_b)

    def slopes(some):
        @pl.loop(*some)
        def _(i):
            for h, part in heads:
                dp = lax.dot_general(g[h], flat[keys(i), 128:], NT, preferred_element_type=F32)
                d = (big[slot_of(h, i), :] * over[h] * (dp - w[h]) * FACTOR).astype(BF16)
                part[...] += jnp.dot(d, flat[keys(i), :128], preferred_element_type=F32)

    slopes((0, count // 2))
    step((wo_sum,))
    step(mixes)
    step((g_share, q_share))
    slopes((count // 2, count))
    step((g_share, q_share))
    for h, part in heads:
        dq[:, h * 128:(h + 1) * 128] = part[...].astype(BF16)
        for j, v in enumerate((m[h], over[h], w[h])):
            table = jnp.where(lane == 3 * h + j, v, table)
    own_stats[...] = table.T[:8, :]
    told = [net.push(own_stats, stats.at[r], p) for p in peers]
    stats[r] = own_stats[...]

    @pl.loop(0, 16)
    def _(i):
        big[lot(0, i, 256), :] = jnp.dot(norm_t[i], dq[...], preferred_element_type=F32)

    wq_sum = scatter_row(s_lane, lambda x, k: big.at[lot(0, 2 * x + k)], *rows[1], put_wq)
    start(wq_sum)
    step((wo_sum,))
    while q_share in live or g_share in live:
        step((q_share, g_share))
    for copy in told:
        copy.wait_recv()

    key = base + lax.broadcasted_iota(jnp.int32, (BLOCK, 1), 0)
    k, v = kv[r, :, :128], kv[r, :, 128:]
    sums = [(ref, at) for at in (0, 128) for ref in (qkv.at[:, pl.ds(at, 128)], qkv.at[:, pl.ds(256 + at, 128)])]
    qkv[...] = jnp.zeros_like(qkv)
    for b in range(5):

        @pl.when(r + b < 8)
        def _():
            o = r + b
            row = o * BLOCK + lax.broadcasted_iota(jnp.int32, (1, BLOCK), 1)
            seen = (key <= row) & (key >= doc_start(row, docs))
            for h in range(2):
                cols = slice(h * 128, (h + 1) * 128)
                more = slice(256 + h * 128, 256 + (h + 1) * 128)
                q, g = qs[o, :, cols], gs[o, :, cols]
                m, over, w = (stats[o, 3 * h + j:3 * h + j + 1, :] for j in range(3))
                s = lax.dot_general(k, q, NT, preferred_element_type=F32) * FACTOR
                p = jnp.exp(jnp.where(seen, s, -1e30) - m) * over
                dp = lax.dot_general(v, g, NT, preferred_element_type=F32)
                d = (p * (dp - w) * FACTOR).astype(BF16)
                qkv[:, more] += jnp.dot(p.astype(BF16), g, preferred_element_type=F32)
                qkv[:, cols] += jnp.dot(d, q, preferred_element_type=F32)

        if b == 0:
            step(mixes)
        if b == 2:
            step((wq_sum,))
            step(mixes)

    two = [qkv[:, at:at + 128].astype(BF16).astype(F32) + qkv[:, at + 128:at + 256].astype(BF16).astype(F32)
           for at in (0, 256)]
    for j, value in enumerate(two):
        upper = value.astype(BF16)
        dkv[:, j * 128:(j + 1) * 128] = upper
        dkv[:, 256 + j * 128:256 + (j + 1) * 128] = (value - upper.astype(F32)).astype(BF16)
    even = lax.rem(c, 2) == 0
    left = jnp.concatenate([two[0][:, :64], two[1][:, :64]], axis=1)
    right = jnp.concatenate([two[0][:, 64:], two[1][:, 64:]], axis=1)
    keep[...] = jnp.where(even, left, right)
    give[...] = jnp.where(even, right, left)
    swap = net.push(give, got, (r, c + 1 - 2 * lax.rem(c, 2)))

    own_grad[...] = grad3[c]
    net.finish(gathered)
    ngrad = grad3
    part_a[...] = jnp.zeros_like(part_a)
    for piece in range(2):

        @pl.loop(4 * piece, 4 * piece + 4)
        def _(i):
            for j in range(2):
                at = pl.ds(j * 256, 256)
                g = lax.dot_general(dq[...], wqkv[i, at, :256], NT, preferred_element_type=F32)
                for h in range(2):
                    g += lax.dot_general(dkv[:, h * 256:(h + 1) * 256], wqkv[i, at, 256:], NT,
                                         preferred_element_type=F32)
                ngrad[2 * i + j] = g.astype(BF16)
                a = g * tok3[2 * i + j, :BLOCK, :].astype(F32)
                part_a[...] += fold(a * tok3[2 * i + j, BLOCK:BLOCK + 1, :].astype(F32))
                a = a * jnp.concatenate([inv[...], inv[...]], axis=1)
                gain[2 * i + j] = jnp.broadcast_to(jnp.sum(a, axis=0, keepdims=True), (8, WIDTH))

        step((wq_sum,) if piece == 0 else (wo_sum,))

    inner[...] = jnp.broadcast_to(jnp.sum(part_a[...].T, axis=0, keepdims=True), inner.shape)
    small = []
    for d, dev in enumerate(others):
        small.append(net.push(gain.at[lax.rem(c + d + 1, 16), pl.ds(0, 1)], gains.at[d, pl.ds(0, 1)], dev))
        small.append(net.push(inner.at[pl.ds(0, 1)], inners.at[d, pl.ds(0, 1)], dev))
    earlier = net.total
    n_lane = Lane(net, g_lane)
    ngs = (scatter_plane(n_lane, ngrad, *planes[2], 0, 112, "y", put_grad),
           scatter_plane(n_lane, ngrad, *planes[3], 224, 112, "z", put_grad))
    start(*ngs)
    swap.wait_recv()
    four = keep[...] + got[...]
    upper = four.astype(BF16)
    dkv[:, :128] = upper
    dkv[:, 128:256] = (four - upper.astype(F32)).astype(BF16)

    @pl.loop(0, 4)
    def _(i):
        for j in range(4):
            t = jnp.dot(norm_t[4 * i + j], dkv[:, :256], preferred_element_type=F32)
            rows_at = pl.ds(pl.multiple_of(4096 + (j % 2) * 256 + i * 512, 256), 256)
            big[rows_at, (j // 2) * 128:(j // 2) * 128 + 128] = fold(t)

    e_lane = Lane(net, o_lane, k_lane)
    kv_sum = scatter_row(e_lane, lambda x, k: big.at[lot(4096, x), pl.ds(pl.multiple_of(k * 128, 128), 128)],
                         *rows[2], put_kv)
    start(kv_sum)
    for some in (mixes, ngs, (kv_sum,)):
        step(some)
    for copy in small:
        copy.wait_recv()
    g, total = gain[c, 0:1, :], inner[0:1, :]
    for d in range(15):
        g = g + gains[d, 0:1, :]
        total = total + inners[d, 0:1, :]
    gain_all[...] = jnp.broadcast_to(g, gain_all.shape)
    final = [e_lane.push(gain_all.at[pl.ds(0, 1)], gain_rows.at[d, pl.ds(0, 1)], dev) for d, dev in enumerate(peers)]
    net.finish(earlier)
    for some in ((wo_sum,), (wq_sum,), (kv_sum,), ngs, (kv_sum,), (wq_sum,), ngs):
        step(some)
    while live:
        step()
    for copy in final:
        copy.wait_recv()
    for d in range(7):
        g = g + gain_rows[d, 0:1, :]
    gain_grad[...] = g
    mean = jnp.broadcast_to(total, (128, BLOCK)).T * (1.0 / 4096)
    mean = jnp.concatenate([mean, mean], axis=1)
    i = jnp.concatenate([inv[...], inv[...]], axis=1)
    scaled = token_grad[...] * tok3[c, BLOCK:BLOCK + 1, :].astype(F32)
    token_grad[...] = own_grad[...].astype(F32) + i * scaled - tok3[c, :BLOCK, :].astype(F32) * i**3 * mean
    for copy in outs:
        copy.wait()
    net.finish()


def whole_layer(*operands):
    copies = 4 * 30 + 21 + 4 * 11 + 7 + 1 + 30
    scratch = [
        ((16, BLOCK + EXTRA, WIDTH), BF16), ((16, BLOCK, WIDTH), BF16), ((8, 512, 512), BF16), ((8, 256, 512), BF16),
        ((16, WIDTH, BLOCK), BF16), ((8, BLOCK, 256), BF16), ((8, BLOCK, 256), BF16), ((8, BLOCK, 256), BF16),
        ((20 * BLOCK + 4096, 256), F32), ((16, BLOCK, WIDTH), BF16), ((BLOCK, WIDTH), BF16),
        ((BLOCK, 128), F32), ((BLOCK, 128), F32), ((BLOCK, 128), F32), ((BLOCK, 512), F32), ((BLOCK, 512), BF16),
        ((BLOCK, 256), BF16), ((256, BLOCK), BF16), ((BLOCK, 256), BF16), ((BLOCK, 128), F32), ((BLOCK, 128), F32),
        ((BLOCK, 128), F32), ((8, BLOCK), F32), ((8, 8, BLOCK), F32), ((16, 8, WIDTH), F32), ((8, BLOCK), F32),
        ((15, 8, WIDTH), F32), ((15, 8, BLOCK), F32), ((8, WIDTH), F32), ((7, 8, WIDTH), F32),
    ] + PLANE_SCRATCH * 4 + row_scratch(256) * 2 + row_scratch(128)
    return pl.pallas_call(
        whole_kernel,
        out_shape=[
            jax.ShapeDtypeStruct((BLOCK, WIDTH), BF16), jax.ShapeDtypeStruct((BLOCK, WIDTH), F32),
            jax.ShapeDtypeStruct((1, WIDTH), F32), jax.ShapeDtypeStruct((512, 256), F32),
            jax.ShapeDtypeStruct((64, 512), F32), jax.ShapeDtypeStruct((64, 512), F32),
            jax.ShapeDtypeStruct((256, 512), F32),
        ],
        in_specs=[SMEM, ANY, VM] + [ANY] * 5,
        out_specs=[VM, VM, VM, ANY, VM, VM, ANY],
        scratch_shapes=[pltpu.VMEM(*b) for b in scratch] + [
            pltpu.SemaphoreType.DMA((POOL,)), pltpu.SemaphoreType.DMA((copies,)), pltpu.SemaphoreType.DMA((6,)),
            pltpu.SemaphoreType.DMA((3,))],
        compiler_params=pltpu.CompilerParams(collective_id=1, has_side_effects=True, vmem_limit_bytes=VMEM_MOST),
        name="whole_layer",
    )(*operands)


def hand_kernel(*refs):
    srcs, dsts, bufs = refs[:7], refs[7:14], refs[14:21]
    sems, more = refs[21:]
    legs = [pltpu.make_async_copy(src, buf, sems.at[i]) for i, (src, buf) in enumerate(zip(srcs, bufs))]
    outs = [pltpu.make_async_copy(buf, dst, more.at[i]) for i, (buf, dst) in enumerate(zip(bufs, dsts))]
    for copy in legs:
        copy.start()
    for leg, out in zip(legs, outs):
        leg.wait()
        out.start()
    for copy in outs:
        copy.wait()


def hand_over(*arrays):
    return pl.pallas_call(
        hand_kernel,
        out_shape=[jax.ShapeDtypeStruct(a.shape, a.dtype) for a in arrays],
        in_specs=[ANY] * 7,
        out_specs=[ANY] * 7,
        scratch_shapes=[pltpu.VMEM(a.shape, a.dtype) for a in arrays] + [pltpu.SemaphoreType.DMA((7,))] * 2,
        name="hand_over",
    )(*arrays)


def body(tokens, norm_gain, w_query, w_key, w_value, w_out, out_grad, doc_lengths):
    layer_out, token_grad, gain_grad, wq_grad, wk_grad, wv_grad, wo_grad = hand_over(*whole_layer(
        doc_lengths, tokens, norm_gain, out_grad, w_query, w_key, w_value, w_out))
    return layer_out, token_grad, gain_grad.reshape(WIDTH), wq_grad, wk_grad.T, wv_grad.T, wo_grad


def solution(mesh):
    in_specs = (P("row", "col"), P("col"), P("row", "col"), P("row", None), P("row", None),
                P("col", "row"), P("row", "col"), P())
    out_specs = (P("row", "col"), P("row", "col"), P("col"), P("row", "col"), P("row", "col"),
                 P("row", "col"), P("col", "row"))
    return jax.shard_map(body, mesh=mesh, in_specs=in_specs, out_specs=out_specs, check_vma=False)
```
